32 devices in a mesh: groups: 2 (over y), ctx: 4 (over z), fsdp: 2 (over x), sub: 2 (over core).
Axes of the slice: x: 2, y: 2, z: 4, core: 2. Of those that a mesh axis runs over, the one named last changes fastest.
Arguments:
- streams: bfloat16 [3, 2048, 4096], P(None, ('groups', 'ctx', 'sub'), 'fsdp'), parts along dimension 1, may hold values from -6 to 6
- feat_taps: float32 [3, 7, 4096], P(None, None, 'fsdp'), may hold values from -2.4 to 2.4
- long_filter: bfloat16 [128, 4096], P('ctx', 'fsdp'), may hold values from -0.5 to 0.5
- upstream: bfloat16 [2048, 4096], P(('groups', 'ctx', 'sub'), 'fsdp'), parts along dimension 0, may hold values from -6 to 6
- score_dir: float32 [4096], P('fsdp'), may hold values from -21 to 21
- seg_lengths: int32 [16], P('groups'), parts along dimension 0, may hold values from 1 to 512, 1024 in all
- list_ids: int32 [16], P('groups'), parts along dimension 0, may hold values from 0 to 1
Outputs:
- d_streams: bfloat16 [3, 2048, 4096], P(None, ('groups', 'ctx', 'sub'), 'fsdp'), parts along dimension 1
- d_feat: float32 [6, 7, 4096], P('groups', None, 'fsdp'), parts along dimension 0
- d_filter: float32 [256, 4096], P(('groups', 'ctx'), 'fsdp'), parts along dimension 0
The draws below stay inside these ranges and needn't reach their ends.
There are 2 independent parts, one for each index of `groups`. The reference program is written for one: setup_inputs(seed, part) draws one part's arguments, and reference() takes and returns one part's arrays. A program takes and returns all parts, laid end to end along the dimension named above; an argument that names none is the same for every part. Nothing has to cross between parts.
Inputs may be any that keep to these rules, and one draw needn't show every extreme that they name: `seg_lengths`: the lengths sum to 1024 and the longest segment has exactly 512 tokens.
All inputs are finite; a program needn't handle non-finite values.
Results may differ from the reference program's by a relative error of at most 0.012.
Values may be sent and summed in bfloat16 or wider, within the bound.
A program may use at most 64 MiB of HBM per device.

```python
import math
import jax
import jax.numpy as jnp
import numpy as np
from jax import lax

C = 4096
LH = 128
KF = 7
TOKENS = 1024
SEGS = 8
MOST = 512
LISTS = 2


def with_ends(array, stream_key, smallest, top_value):
    extent = array.shape
    spot = [jax.random.randint(jax.random.fold_in(stream_key, axis), (), 0, extent[axis]) for axis in range(len(extent))]
    array = array.at[tuple(spot)].set(smallest)
    longest = extent.index(max(extent))
    spot[longest] = (spot[longest] + 1) % extent[longest]
    return array.at[tuple(spot)].set(top_value)


def steps_of(key, shape, pieces, smallest, top_value):
    level, own = 1.0, jax.random.fold_in(key, 6)
    for axis_at, blocks in pieces:
        steps = jnp.exp(jax.random.uniform(jax.random.fold_in(own, axis_at), (blocks,), jnp.float32, smallest / len(pieces), top_value / len(pieces)))
        level = level * jnp.repeat(steps, shape[axis_at] // blocks).reshape([-1 if axis == axis_at else 1 for axis in range(len(shape))])
    return level


def profile(count, total, limit, skew):
    portions = [(1 << 20) // math.isqrt(rank ** skew) + 1 for rank in range(2, count + 1)]
    spare, given = total - limit - (count - 1), [1] * (count - 1)
    while spare > 0:
        free = [i for i in range(count - 1) if given[i] < limit]
        pool, budget = sum([portions[i] for i in free]), spare
        for i in free:
            addition = min(limit - given[i], max(1, budget * portions[i] // pool), spare)
            given[i] = given[i] + addition
            spare = spare - addition
    return np.array([limit] + given)


def uneven_parts(own_key, amount, total, reach, lean):
    if amount == 2:
        one = jax.random.randint(own_key, (), max(1, total - reach), min(reach, total - 1) + 1)
        return jnp.stack([one, total - one])
    sizes = jnp.asarray(profile(amount, total, reach, lean), jnp.int32)
    pairs = (amount - 1) // 2
    source_of, taker = sizes[1:1 + 2 * pairs:2], sizes[2:2 + 2 * pairs:2]
    margin = jnp.minimum(source_of - 1, reach - taker)
    shifted = jax.random.randint(jax.random.fold_in(own_key, 1), (pairs,), 0, 1 << 20) % (margin + 1)
    sizes = sizes.at[1:1 + 2 * pairs:2].set(source_of - shifted).at[2:2 + 2 * pairs:2].set(taker + shifted)
    return sizes[jax.random.permutation(jax.random.fold_in(own_key, 2), amount)]


def gaussian(own_key, shape, spread, bound, shards=(), kind=jnp.bfloat16):
    values = jax.random.normal(own_key, shape, jnp.float32) * spread
    if len(shards) > 0:
        values = steps_of(own_key, shape, shards, -0.22, 0.18) * values
    return jnp.clip(values, min=-bound, max=bound).astype(kind)


def setup_inputs(seed: int = 0, part: int = 0) -> dict:
    keys = jax.random.split(jax.random.key(seed), 8)
    own_keys = jax.random.split(jax.random.fold_in(keys[7], part), 8)
    return {
        "streams": gaussian(own_keys[0], (3, TOKENS, C), 1.0, 6.0, ((1, 8), (2, 2))),
        "feat_taps": gaussian(keys[1], (3, KF, C), 0.4, 2.4, ((2, 2),), jnp.float32),
        "long_filter": gaussian(keys[2], (LH, C), LH ** -0.5, 0.5, ((0, 4), (1, 2))),
        "upstream": gaussian(own_keys[3], (TOKENS, C), 1.0, 6.0, ((0, 8), (1, 2))),
        "score_dir": gaussian(keys[4], (C,), 3.5, 21.0, ((0, 2),), jnp.float32),
        "seg_lengths": uneven_parts(own_keys[5], SEGS, TOKENS, MOST, 2).astype(jnp.int32),
        "list_ids": with_ends(jax.random.randint(own_keys[6], (SEGS,), 0, LISTS), jax.random.fold_in(own_keys[6], 1), 0, LISTS - 1).astype(jnp.int32),
    }


HIGH = lax.Precision.HIGHEST


def tap_block(tap_count):
    return 16 if tap_count % 16 == 0 else tap_count


def segment_age(seg_lengths, positions):
    offsets = jnp.cumsum(seg_lengths, dtype=jnp.int32) - seg_lengths
    member = offsets[None, :] <= positions[:, None]
    seg_index = jnp.sum(member.astype(jnp.int32), axis=1, dtype=jnp.int32) - 1
    seg_start = jnp.max(jnp.where(member, offsets[None, :], 0), axis=1)
    return seg_index, (positions - seg_start).astype(jnp.int32)


def causal_taps(tap_table, extended, row_age, tok_rows):
    tap_count = tap_table.shape[0]
    per_turn = tap_block(tap_count)

    def advance(b, running):
        for m in range(per_turn):
            j = b * per_turn + m
            window = lax.dynamic_slice_in_dim(extended, tap_count - 1 - j, tok_rows, 0)
            weight_row = lax.dynamic_index_in_dim(tap_table, j, 0, keepdims=False)
            running = running + jnp.where((row_age >= j)[:, None], weight_row[None, :] * window.astype(jnp.float32), 0.0)
        return running

    start_sum = jnp.zeros((tok_rows, extended.shape[1]), jnp.float32)
    return lax.fori_loop(0, tap_count // per_turn, advance, start_sum)


def reverse_taps(tap_table, extended, ext_age, tok_rows):
    tap_count = tap_table.shape[0]
    per_turn = tap_block(tap_count)

    def advance(b, running):
        for m in range(per_turn):
            j = b * per_turn + m
            window = lax.dynamic_slice_in_dim(extended, j, tok_rows, 0)
            keep = lax.dynamic_slice_in_dim(ext_age, j, tok_rows, 0) >= j
            weight_row = lax.dynamic_index_in_dim(tap_table, j, 0, keepdims=False)
            running = running + jnp.where(keep[:, None], weight_row[None, :] * window.astype(jnp.float32), 0.0)
        return running

    start_sum = jnp.zeros((tok_rows, extended.shape[1]), jnp.float32)
    return lax.fori_loop(0, tap_count // per_turn, advance, start_sum)


def correlate_taps(gradient, extended, row_age, tap_count, tok_rows):
    per_turn = tap_block(tap_count)

    def advance(b, result):
        collected = []
        for m in range(per_turn):
            j = b * per_turn + m
            window = lax.dynamic_slice_in_dim(extended, tap_count - 1 - j, tok_rows, 0)
            product = gradient.astype(jnp.float32) * window.astype(jnp.float32)
            collected.append(jnp.sum(jnp.where((row_age >= j)[:, None], product, 0.0), axis=0))
        return lax.dynamic_update_slice_in_dim(result, jnp.stack(collected), b * per_turn, 0)

    start_rows = jnp.zeros((tap_count, gradient.shape[1]), jnp.float32)
    return lax.fori_loop(0, tap_count // per_turn, advance, start_rows)


def list_coef(totals, seg_lengths, list_ids):
    length_f = seg_lengths.astype(jnp.float32)
    scores = totals / length_f
    mates = (list_ids[:, None] == list_ids[None, :]).astype(jnp.float32)
    mean_score = jnp.dot(mates, scores, precision=HIGH) / jnp.sum(mates, axis=1)
    return (scores - mean_score) / length_f


def reference(streams, feat_taps, long_filter, upstream, score_dir, seg_lengths, list_ids):
    tok_rows = streams.shape[1]
    positions = jnp.arange(tok_rows, dtype=jnp.int32)
    seg_index, row_age = segment_age(seg_lengths, positions)
    age_span = jnp.concatenate([row_age, jnp.zeros((LH - 1,), jnp.int32)])
    front = [jnp.pad(streams[i], ((KF - 1, 0), (0, 0))) for i in range(3)]
    featured = [causal_taps(feat_taps[i], front[i], row_age, tok_rows).astype(jnp.bfloat16) for i in range(3)]
    query, key_feat, value_feat = featured
    product = (key_feat.astype(jnp.float32) * value_feat.astype(jnp.float32)).astype(jnp.bfloat16)
    filt = long_filter.astype(jnp.float32)
    prod_ext = jnp.pad(product, ((LH - 1, 0), (0, 0)))
    mixed = causal_taps(filt, prod_ext, row_age, tok_rows)
    out_y = query.astype(jnp.float32) * mixed
    projected = jnp.dot(out_y, score_dir, precision=HIGH)
    onehot = (seg_index[:, None] == jnp.arange(SEGS, dtype=jnp.int32)[None, :]).astype(jnp.float32)
    totals = jnp.dot(projected, onehot, precision=HIGH)
    coef = list_coef(totals, seg_lengths, list_ids)
    tok_coef = jnp.dot(onehot, coef, precision=HIGH)
    d_out = upstream.astype(jnp.float32) + tok_coef[:, None] * score_dir[None, :]
    d_query = (d_out * mixed).astype(jnp.bfloat16)
    d_mixed = (d_out * query.astype(jnp.float32)).astype(jnp.bfloat16)
    dm_ext = jnp.pad(d_mixed, ((0, LH - 1), (0, 0)))
    d_prod = reverse_taps(filt, dm_ext, age_span, tok_rows)
    d_key = (d_prod * value_feat.astype(jnp.float32)).astype(jnp.bfloat16)
    d_value = (d_prod * key_feat.astype(jnp.float32)).astype(jnp.bfloat16)
    d_filter = correlate_taps(d_mixed, prod_ext, row_age, LH, tok_rows)
    grads = [d_query, d_key, d_value]
    d_streams = []
    d_feat = []
    for i in range(3):
        grad_ext = jnp.pad(grads[i], ((0, KF - 1), (0, 0)))
        d_streams.append(reverse_taps(feat_taps[i], grad_ext, age_span, tok_rows).astype(jnp.bfloat16))
        d_feat.append(correlate_taps(grads[i], front[i], row_age, KF, tok_rows))
    return jnp.stack(d_streams), jnp.stack(d_feat), d_filter
```

```python
import functools

import jax
import jax.numpy as jnp
import numpy as np
from jax import lax
from jax.experimental import pallas as pl
from jax.experimental.pallas import tpu as pltpu
from jax.sharding import PartitionSpec as P

LH = 128
KF = 7
R = 128
F32 = jnp.float32
BF16 = jnp.bfloat16
MESH = pl.DeviceIdType.MESH

LEVELS = (64, 32, 16, 8, 4, 2, 1)
ROWS = 2 * LH + 128 * len(LEVELS)


def wave(m, positions):
    angle = np.pi * np.outer(2 * np.arange(m) + 1, positions) / (2 * m)
    return np.cos(angle), -np.sin(angle)


def tables():
    first, second, taps, out_first, out_second, out_taps = [], [], [], [], [], []
    for m in (LH,) + LEVELS:
        pairs = max(1, R // (2 * m))
        early, late, every = wave(m, np.arange(m)), wave(m, np.arange(m, 2 * m)), wave(m, np.arange(2 * m))
        span = min(2 * m, LH)
        for part in (0, 1):
            both = np.zeros((2, pairs * m, R))
            for g in range(pairs):
                rows = slice(g * m, (g + 1) * m)
                start = 2 * m * g
                both[0, rows, start : start + m] = early[part]
                both[1, rows, start + m if m < LH else 0 : start + 2 * m if m < LH else LH] = late[part]
            first.append(both[0])
            second.append(both[1])
            out_first.append(both[0].T / m)
            out_second.append(both[1].T / m)
            lag = np.zeros((m, LH))
            lag[:, 1:span] = every[part][:, 1:span]
            out_taps.append(np.tile(lag, (pairs, 1)).T / m)
            taps.append(np.tile(lag, (max(1, 16 // m), 1)))
    return (
        np.concatenate(first, 0), np.concatenate(second, 0), np.concatenate(taps, 0),
        np.concatenate(out_second, 1), np.concatenate(out_first, 1), np.concatenate(out_taps, 1),
    )


TABLES = [t.astype(np.float32) for t in tables()]
TAP_ROWS = TABLES[2].shape[0]


def starts(lens_ref):
    offsets, off = [], jnp.int32(0)
    for s in range(lens_ref.shape[0]):
        offsets.append(off)
        off = off + lens_ref[s]
    return offsets


def segment_of(offsets, position):
    seg = jnp.where(offsets[0] <= position, 0, -1)
    for off in offsets[1:]:
        seg = seg + jnp.where(off <= position, 1, 0)
    return seg


def age_of(offsets, position):
    start = jnp.zeros(position.shape, jnp.int32)
    for off in offsets:
        start = jnp.where(off <= position, off, start)
    return position - start


def down(rows):
    return lax.broadcasted_iota(jnp.int32, (rows, 1), 0)


def across(columns):
    return lax.broadcasted_iota(jnp.int32, (1, columns), 1)


def dot(a, b):
    return jnp.dot(a, b, preferred_element_type=F32)


def send(src, dst, sems, device):
    return pltpu.make_async_remote_copy(
        src_ref=src, dst_ref=dst, send_sem=sems[0], recv_sem=sems[1], device_id=device,
        device_id_type=MESH,
    )


def wide(row):
    return jnp.broadcast_to(row, (16, row.shape[1])).astype(BF16)


def scaled(tile, block):
    rows, width = block.shape
    return (block.reshape(rows // 16, 16, width) * tile[None]).reshape(rows, width)


def tap_parts(hat_ref, cols):
    parts, at = [], 0
    for m in (LH,) + LEVELS:
        rows, want = max(m, 16), max(64, m)
        pair = []
        for _ in range(2):
            piece = hat_ref[at : at + rows, cols]
            pair.append(piece if rows == want else jnp.concatenate([piece] * (want // rows), 0))
            at += rows
        parts.append(pair)
    return parts


def level_rows():
    spans, at = [], 0
    for m in (LH,) + LEVELS:
        half = max(64, m)
        spans.append((at, half))
        at += 2 * half
    return spans


def body(
    sizes, width,
    lens_ref, ids_ref, x_hbm, taps_hbm, fil_hbm, up_hbm, dir_ref,
    first_ref, second_ref, ftaps_ref, osecond_ref, ofirst_ref, otaps_ref,
    dx_ref, dtaps_ref, out_ref,
    x_ref, taps_ref, all_ref, up_ref, upn_ref, feat_ref, z_ref, prev_ref, qn_ref, da_ref, w_ref,
    hf_ref, hz_ref, own_first, prev_first, own_second, edge_second, next_second, inv_w, inv_d,
    fwd_ref, bwd_ref, shift_ref, stack_ref, prod_ref, cor_ref, proj_ref, coef_ref,
    part_ref, slots, fil_ref, dfil_ref, tap_ref, fil_a, fil_b, fil_c, fil_sum, tap_a, tap_b, tap_c, tap_sum,
    load_sem, rim_sem, fil_sem, swap_sem, up_sem, z_sem, q_sem, sum_send, sum_recv, halo_sem,
    a_sem, b_sem, c_sem,
):
    n_ctx, n_fsdp, n_sub = sizes
    group, ctx = lax.axis_index("groups"), lax.axis_index("ctx")
    fsdp, sub = lax.axis_index("fsdp"), lax.axis_index("sub")
    chans = dir_ref.shape[1]
    half = chans // 2
    blocks = chans // width
    shard = fil_hbm.shape[0]
    segs = lens_ref.shape[0]
    line = ctx * 2 + sub
    base = line * R
    left = (group, (line - 1) // 2, fsdp, 1 - sub)
    right = (group, (line + 1) // 2, fsdp, 1 - sub)
    partner = (group, ctx, fsdp, 1 - sub)
    has_left, has_right = line > 0, line < 2 * n_ctx - 1
    count = n_ctx * n_fsdp * n_sub
    me = (ctx * n_fsdp + fsdp) * n_sub + sub

    def where(r):
        peer = lax.rem(me + r, count)
        return (
            group, peer // (n_fsdp * n_sub), lax.rem(peer // n_sub, n_fsdp), lax.rem(peer, n_sub),
        )

    kept = pl.ds(pl.multiple_of(sub * half, half), half)
    given = pl.ds(pl.multiple_of((1 - sub) * half, half), half)

    def columns(b):
        return pl.ds(pl.multiple_of(b * width, width), width)

    loads = [
        pltpu.make_async_copy(x_hbm, x_ref.at[:, pl.ds(16, R), :], load_sem.at[0]),
        pltpu.make_async_copy(taps_hbm, taps_ref, load_sem.at[1]),
        pltpu.make_async_copy(fil_hbm, all_ref.at[ctx], load_sem.at[2]),
        pltpu.make_async_copy(up_hbm, up_ref, load_sem.at[3]),
    ]
    for load in loads:
        load.start()

    barrier = pltpu.get_barrier_semaphore()

    def greet(r, carry):
        pl.semaphore_signal(barrier, inc=1, device_id=where(r), device_id_type=MESH)
        return carry

    lax.fori_loop(1, count, greet, 0)

    def rim_copy():
        return send(
            x_hbm.at[:, pl.ds(R - 16, 16), :], x_ref.at[:, pl.ds(0, 16), :],
            (rim_sem.at[0], rim_sem.at[1]), right,
        )

    def up_copy():
        return send(up_hbm, upn_ref, (up_sem.at[0], up_sem.at[1]), left)

    def fil_copy(r):
        return send(
            fil_hbm.at[:, kept], all_ref.at[ctx, :, kept], (fil_sem.at[0, r], fil_sem.at[1, r]),
            (group, lax.rem(ctx + r, n_ctx), fsdp, sub),
        )

    def swap_copy(r):
        held = lax.rem(ctx - r + n_ctx, n_ctx)
        return send(
            all_ref.at[held, :, kept], all_ref.at[held, :, kept],
            (swap_sem.at[0, r], swap_sem.at[1, r]), partner,
        )

    def z_copy(b):
        cols = columns(b)
        return send(
            z_ref.at[:, cols], prev_ref.at[:, cols], (z_sem.at[0, b], z_sem.at[1, b]), right
        )

    def q_copy(b):
        cols = columns(b)
        return send(
            feat_ref.at[0, :, cols], qn_ref.at[:, cols], (q_sem.at[0, b], q_sem.at[1, b]), left
        )

    def halo_copy(b):
        cols = columns(b)
        return send(
            da_ref.at[:, pl.ds(0, 16), cols], da_ref.at[:, pl.ds(R, 16), cols],
            (halo_sem.at[0, b], halo_sem.at[1, b]), left,
        )

    offsets = starts(lens_ref)
    age_down = age_of(offsets, base + down(R))
    age_over = age_of(offsets, base + across(R))
    gap = across(R) - down(R)
    lane = across(R)
    rim_gap = jnp.where(lane < 16 * KF, lane % 16 - 16 + lane // 16, 4 * R) - down(R)
    halo_age = age_of(offsets, base + R + lane % 16)
    halo_gap = jnp.where(lane < 16 * KF, lane % 16 + R - lane // 16, 4 * R) - down(R)
    for j in range(KF):
        span = slice(j * R, (j + 1) * R)
        fwd_ref[:, span] = jnp.where((gap == -j) & (age_down >= j), 1.0, 0.0).astype(BF16)
        bwd_ref[:, span] = jnp.where((gap == j) & (age_over >= j), 1.0, 0.0).astype(BF16)
        wide_gap = across(R + 16) - down(R) - 16
        shift_ref[span, :] = jnp.where((wide_gap == -j) & (age_down >= j), 1.0, 0.0).astype(BF16)
    span = slice(KF * R, (KF + 1) * R)
    fwd_ref[:, span] = jnp.where((rim_gap == 0) & (age_down >= lane // 16), 1.0, 0.0).astype(BF16)
    bwd_ref[:, span] = jnp.where((halo_gap == 0) & (halo_age >= lane // 16), 1.0, 0.0).astype(BF16)
    stack_ref[:, KF * (R + 16) :, :] = jnp.zeros((3, R - 16 * KF, width), BF16)

    def kept_rows(table, mask):
        return jnp.where(mask, table.astype(F32), 0.0).astype(BF16)

    seg_down = segment_of(offsets, base + down(R))
    seg_over = segment_of(offsets, base + lane)
    seg_here, seg_next = segment_of(offsets, base + down(1)), segment_of(offsets, base + R + down(1))
    prev_mask = segment_of(offsets, base - R + lane) == seg_here
    next_mask = segment_of(offsets, base + R + lane) == seg_next
    prev_first[...] = kept_rows(first_ref[: 2 * LH], prev_mask)
    edge_second[...] = kept_rows(second_ref[: 2 * LH], seg_over == seg_here)
    next_second[...] = kept_rows(second_ref[: 2 * LH], next_mask)
    inv_w[:, : 2 * LH] = kept_rows(osecond_ref[:, : 2 * LH], seg_down == seg_here)
    inv_d[:, : 2 * LH] = kept_rows(ofirst_ref[:, : 2 * LH], seg_down == seg_next)
    for i, m in enumerate(LEVELS):
        at, to = 2 * LH + 128 * i, 128 * i
        mask = segment_of(offsets, base + lane // (2 * m) * (2 * m) + m) == seg_over
        own_first[to : to + 128] = kept_rows(first_ref[at : at + 128], mask)
        own_second[to : to + 128] = kept_rows(second_ref[at : at + 128], mask)
        mask = segment_of(offsets, base + down(R) // (2 * m) * (2 * m) + m) == seg_down
        inv_w[:, at : at + 128] = kept_rows(osecond_ref[:, at : at + 128], mask)
        inv_d[:, at : at + 128] = kept_rows(ofirst_ref[:, at : at + 128], mask)

    pl.semaphore_wait(barrier, count - 1)

    @pl.when(has_right)
    def _():
        rim_copy().start()

    for r in range(1, n_ctx):
        fil_copy(r).start()

    @pl.when(has_left)
    def _():
        up_copy().start()

    @pl.when(jnp.logical_not(has_left))
    def _():
        x_ref[:, 0:16, :] = jnp.zeros((3, 16, chans), BF16)
        prev_ref[...] = jnp.zeros(prev_ref.shape, BF16)

    @pl.when(jnp.logical_not(has_right))
    def _():
        upn_ref[...] = jnp.zeros(upn_ref.shape, BF16)
        qn_ref[...] = jnp.zeros(qn_ref.shape, BF16)
        da_ref[:, R:, :] = jnp.zeros((3, 16, chans), BF16)

    for load in loads:
        load.wait()

    @pl.when(has_left)
    def _():
        rim_copy().wait_recv()

    def stacked(i, source, near, far, cols):
        for j in range(KF):
            tile = wide(taps_ref[i, j : j + 1, cols])
            stack_ref[i, j * R : (j + 1) * R, :] = scaled(tile, source[i, near, cols])
            at = KF * R + 16 * j
            stack_ref[i, at : at + 16, :] = scaled(tile, source[i, far, cols])
        return stack_ref[i]

    def feat_block(b, carry):
        cols = columns(b)
        feats = [None] * 3
        for i in (1, 2, 0):
            feats[i] = dot(fwd_ref[...], stacked(i, x_ref, slice(16, 16 + R), slice(0, 16), cols)).astype(BF16)
            feat_ref[i, :, cols] = feats[i]
        z = (feats[1].astype(F32) * feats[2].astype(F32)).astype(BF16)
        z_ref[:, cols] = z

        @pl.when(has_right)
        def _():
            z_copy(b).start()

        @pl.when(has_left)
        def _():
            q_copy(b).start()

        hz_ref[2 * LH :, cols] = dot(own_first[...], z).astype(BF16)
        return carry

    lax.fori_loop(0, blocks, feat_block, 0)

    for r in range(1, n_ctx):
        fil_copy(r).wait_recv()
        swap_copy(r).start()
    for r in range(1, n_ctx):
        swap_copy(r).wait_recv()

    def fil_block(b, carry):
        cols = columns(b)
        taps = all_ref[:, :, cols].astype(F32).reshape(LH, width)
        fil_ref[0:8, cols] = taps[0:8]
        hf_ref[:, cols] = dot(ftaps_ref[...], taps.astype(BF16)).astype(BF16)
        return carry

    lax.fori_loop(0, blocks, fil_block, 0)

    proj_ref[...] = jnp.zeros(proj_ref.shape, F32)

    def mix_block(b, carry):
        cols = columns(b)

        @pl.when(has_left)
        def _():
            z_copy(b).wait_recv()

        hz_ref[: 2 * LH, cols] = dot(prev_first[...], prev_ref[:, cols]).astype(BF16)
        for (at, n), (f_re, f_im) in zip(level_rows(), tap_parts(hf_ref, cols)):
            z_re, z_im = hz_ref[at : at + n, cols], hz_ref[at + n : at + 2 * n, cols]
            prod_ref[at : at + n, :] = f_re * z_re - f_im * z_im
            prod_ref[at + n : at + 2 * n, :] = f_re * z_im + f_im * z_re
        w = dot(inv_w[...], prod_ref[...]) + fil_ref[0:1, cols] * z_ref[:, cols].astype(F32)
        w_ref[:, cols] = w
        weighted = feat_ref[0, :, cols].astype(F32) * w * dir_ref[:, cols]
        part = weighted[:, 0:128]
        for c in range(1, width // 128):
            part = part + weighted[:, c * 128 : (c + 1) * 128]
        proj_ref[...] += part
        return carry

    lax.fori_loop(0, blocks, mix_block, 0)

    for s in range(segs):
        part_ref[s : s + 1, :] = jnp.sum(
            jnp.where(seg_down == s, proj_ref[...], 0.0), axis=0, keepdims=True
        )

    def sum_copy(r):
        return send(part_ref, slots.at[r], (sum_send.at[r], sum_recv.at[r]), where(r))

    def begin(r, carry):
        sum_copy(r).start()
        return carry

    def end(r, carry):
        sum_copy(r).wait()
        return carry

    lax.fori_loop(1, count, begin, 0)
    lax.fori_loop(1, count, end, 0)
    slots[0] = part_ref[...]

    def add_slot(i, total):
        return total + slots[lax.rem(me - i + count, count)]

    summed = lax.fori_loop(0, count, add_slot, jnp.zeros(part_ref.shape, F32))
    ids, id_row = jnp.zeros((segs, 1), jnp.int32), jnp.zeros((1, segs), jnp.int32)
    lengths = jnp.zeros((segs, 1), jnp.int32)
    for s in range(segs):
        ids = jnp.where(down(segs) == s, ids_ref[s], ids)
        id_row = jnp.where(across(segs) == s, ids_ref[s], id_row)
        lengths = jnp.where(down(segs) == s, lens_ref[s], lengths)
    lengths = lengths.astype(F32)
    scores = jnp.sum(summed, axis=1, keepdims=True) / lengths
    same = down(segs) == across(segs)
    score_row = jnp.sum(jnp.where(same, scores, 0.0), axis=0, keepdims=True)
    mates = jnp.where(ids == id_row, 1.0, 0.0)
    means = jnp.sum(mates * score_row, axis=1, keepdims=True) / jnp.sum(
        mates, axis=1, keepdims=True
    )
    coef = (scores - means) / lengths
    coef_row = jnp.sum(jnp.where(same, coef, 0.0), axis=0, keepdims=True)
    hot = segment_of(offsets, base + down(2 * R)) == across(segs)
    coef_ref[...] = jnp.sum(jnp.where(hot, coef_row, 0.0), axis=1, keepdims=True)

    @pl.when(has_right)
    def _():
        up_copy().wait_recv()

    def grad_block(b, carry):
        cols = columns(b)

        @pl.when(has_right)
        def _():
            q_copy(b).wait_recv()

        direction = dir_ref[:, cols]
        d_out = up_ref[:, cols].astype(F32) + coef_ref[0:R, :] * direction
        da_ref[0, 0:R, cols] = (d_out * w_ref[:, cols]).astype(BF16)
        dw = (d_out * feat_ref[0, :, cols].astype(F32)).astype(BF16)
        d_next = upn_ref[:, cols].astype(F32) + coef_ref[R:, :] * direction
        dw_next = (d_next * qn_ref[:, cols].astype(F32)).astype(BF16)
        own = dot(own_second[...], dw).astype(BF16)
        edge = dot(edge_second[...], dw).astype(BF16)
        after = dot(next_second[...], dw_next).astype(BF16)
        for (at, n), (f_re, f_im) in zip(level_rows(), tap_parts(hf_ref, cols)):
            if at == 0:
                d_re, d_im, e_re, e_im = after[:n], after[n:], edge[:n], edge[n:]
            else:
                to = at - 2 * LH
                d_re, d_im = own[to : to + n], own[to + n : to + 2 * n]
                e_re, e_im = d_re, d_im
            z_re, z_im = hz_ref[at : at + n, cols], hz_ref[at + n : at + 2 * n, cols]
            prod_ref[at : at + n, :] = f_re * d_re + f_im * d_im
            prod_ref[at + n : at + 2 * n, :] = f_re * d_im - f_im * d_re
            cor_ref[at : at + n, :] = z_re * e_re + z_im * e_im
            cor_ref[at + n : at + 2 * n, :] = z_re * e_im - z_im * e_re
        dw_wide = dw.astype(F32)
        dz = dot(inv_d[...], prod_ref[...]) + fil_ref[0:1, cols] * dw_wide
        da_ref[1, 0:R, cols] = (dz * feat_ref[2, :, cols].astype(F32)).astype(BF16)
        da_ref[2, 0:R, cols] = (dz * feat_ref[1, :, cols].astype(F32)).astype(BF16)
        whole = jnp.sum(dw_wide * z_ref[:, cols].astype(F32), axis=0, keepdims=True)
        dfil = dot(otaps_ref[...], cor_ref[...]) + jnp.where(down(LH) == 0, whole, 0.0)
        dfil_ref[:, :, cols] = dfil.reshape(n_ctx, shard, width).astype(BF16)

        @pl.when(has_left)
        def _():
            halo_copy(b).start()

        return carry

    first = [send(dfil_ref.at[:, :, given], fil_a, (a_sem.at[0, 0], a_sem.at[1, 0]), partner)]
    for i in range(3):
        first.append(
            send(
                tap_ref.at[i, :, given], tap_a.at[i], (a_sem.at[0, 1 + i], a_sem.at[1, 1 + i]),
                partner,
            )
        )

    def second(c, r):
        sems = (b_sem.at[0, c, r], b_sem.at[1, c, r])
        owner = lax.rem(ctx + r, n_ctx)
        target = (group, owner, fsdp, sub)
        if c == 0:
            return send(fil_c.at[owner], fil_b.at[r], sems, target)
        return send(tap_c.at[c - 1], tap_b.at[r, c - 1], sems, target)

    last = [
        send(fil_sum, out_ref.at[:, kept], (c_sem.at[0, 0], c_sem.at[1, 0]), partner),
        send(tap_sum, dtaps_ref.at[:, :, kept], (c_sem.at[0, 1], c_sem.at[1, 1]), partner),
    ]

    per_half = blocks // 2
    lax.fori_loop((1 - sub) * per_half, (2 - sub) * per_half, grad_block, 0)
    first[0].start()
    lax.fori_loop(sub * per_half, (1 + sub) * per_half, grad_block, 0)

    def tap_sums(i):
        def block(b, carry):
            cols = columns(b)
            ext = x_ref[i, :, cols]
            own = da_ref[i, 0:R, cols].astype(F32)
            sums = []
            for j in range(KF):
                moved = dot(shift_ref[j * R : (j + 1) * R, :], ext)
                sums.append(jnp.sum(own * moved, axis=0, keepdims=True))
            sums.append(jnp.zeros((1, width), F32))
            tap_ref[i, :, cols] = jnp.concatenate(sums, axis=0).astype(BF16)
            return carry

        lax.fori_loop(0, blocks, block, 0)

    def stream(i):
        def block(b, carry):
            cols = columns(b)
            dx_ref[i, :, cols] = dot(
                bwd_ref[...], stacked(i, da_ref, slice(0, R), slice(R, R + 16), cols)
            ).astype(BF16)
            return carry

        lax.fori_loop(0, blocks, block, 0)

    def relay(c):
        first[c].wait()
        if c == 0:
            fil_c[...] = (dfil_ref[:, :, kept].astype(F32) + fil_a[...].astype(F32)).astype(BF16)
        else:
            i = c - 1
            tap_c[i] = (tap_ref[i, :, kept].astype(F32) + tap_a[i].astype(F32)).astype(BF16)
        for r in range(1, n_ctx):
            second(c, r).start()

    relay(0)
    tap_sums(0)
    first[1].start()
    tap_sums(1)
    first[2].start()
    relay(1)
    tap_sums(2)
    first[3].start()
    relay(2)

    @pl.when(has_right)
    def _():
        for b in range(blocks):
            halo_copy(b).wait_recv()

    stream(0)
    relay(3)
    stream(1)
    for r in range(1, n_ctx):
        second(0, r).wait()
    total = fil_c[ctx].astype(F32)
    for r in range(1, n_ctx):
        total = total + fil_b[r].astype(F32)
    fil_sum[...] = total
    out_ref[:, kept] = total
    last[0].start()
    stream(2)
    for c in range(1, 4):
        for r in range(1, n_ctx):
            second(c, r).wait()
    tap_b[0] = tap_c[...]

    def add(d, running):
        return running + tap_b[lax.rem(ctx - d + n_ctx, n_ctx)].astype(F32)

    taps_total = lax.fori_loop(0, n_ctx, add, jnp.zeros(tap_sum.shape, F32))
    tap_sum[...] = taps_total
    dtaps_ref[:, :, kept] = taps_total
    last[1].start()

    @pl.when(has_left)
    def _():
        up_copy().wait_send()
        for b in range(blocks):
            q_copy(b).wait_send()
            halo_copy(b).wait_send()

    @pl.when(has_right)
    def _():
        rim_copy().wait_send()
        for b in range(blocks):
            z_copy(b).wait_send()

    for r in range(1, n_ctx):
        fil_copy(r).wait_send()
        swap_copy(r).wait_send()
    last[0].wait()
    last[1].wait()


def local(sizes, streams, feat_taps, long_filter, upstream, score_dir, seg_lengths, list_ids):
    rows, chans = streams.shape[1:]
    assert rows == R
    width = min(512, chans // 2)
    blocks = chans // width
    half = chans // 2
    n_ctx = sizes[0]
    count = sizes[0] * sizes[1] * sizes[2]
    shard = long_filter.shape[0]
    segs = seg_lengths.shape[0]
    vmem = pl.BlockSpec(memory_space=pltpu.VMEM)
    smem = pl.BlockSpec(memory_space=pltpu.SMEM)
    hbm = pl.BlockSpec(memory_space=pl.ANY)
    dma = pltpu.SemaphoreType.DMA
    own = ROWS - 2 * LH
    d_streams, d_taps, d_filter = pl.pallas_call(
        functools.partial(body, sizes, width),
        in_specs=[smem, smem, hbm, hbm, hbm, hbm] + [vmem] * 7,
        out_specs=[vmem] * 3,
        out_shape=[
            jax.ShapeDtypeStruct((3, rows, chans), BF16),
            jax.ShapeDtypeStruct((3, 8, chans), F32),
            jax.ShapeDtypeStruct((shard, chans), F32),
        ],
        scratch_shapes=[
            pltpu.VMEM((3, R + 16, chans), BF16),
            pltpu.VMEM((3, KF, chans), F32),
            pltpu.VMEM((n_ctx, shard, chans), BF16),
            pltpu.VMEM((R, chans), BF16),
            pltpu.VMEM((R, chans), BF16),
            pltpu.VMEM((3, R, chans), BF16),
            pltpu.VMEM((R, chans), BF16),
            pltpu.VMEM((R, chans), BF16),
            pltpu.VMEM((R, chans), BF16),
            pltpu.VMEM((3, R + 16, chans), BF16),
            pltpu.VMEM((R, chans), F32),
            pltpu.VMEM((TAP_ROWS, chans), BF16),
            pltpu.VMEM((ROWS, chans), BF16),
            pltpu.VMEM((own, R), BF16),
            pltpu.VMEM((2 * LH, R), BF16),
            pltpu.VMEM((own, R), BF16),
            pltpu.VMEM((2 * LH, R), BF16),
            pltpu.VMEM((2 * LH, R), BF16),
            pltpu.VMEM((R, ROWS), BF16),
            pltpu.VMEM((R, ROWS), BF16),
            pltpu.VMEM((R, (KF + 1) * R), BF16),
            pltpu.VMEM((R, (KF + 1) * R), BF16),
            pltpu.VMEM((KF * R, R + 16), BF16),
            pltpu.VMEM((3, (KF + 1) * R, width), BF16),
            pltpu.VMEM((ROWS, width), BF16),
            pltpu.VMEM((ROWS, width), BF16),
            pltpu.VMEM((R, 128), F32),
            pltpu.VMEM((2 * R, 1), F32),
            pltpu.VMEM((segs, 128), F32),
            pltpu.VMEM((count, segs, 128), F32),
            pltpu.VMEM((8, chans), F32),
            pltpu.VMEM((n_ctx, shard, chans), BF16),
            pltpu.VMEM((3, 8, chans), BF16),
            pltpu.VMEM((n_ctx, shard, half), BF16),
            pltpu.VMEM((n_ctx, shard, half), BF16),
            pltpu.VMEM((n_ctx, shard, half), BF16),
            pltpu.VMEM((shard, half), F32),
            pltpu.VMEM((3, 8, half), BF16),
            pltpu.VMEM((n_ctx, 3, 8, half), BF16),
            pltpu.VMEM((3, 8, half), BF16),
            pltpu.VMEM((3, 8, half), F32),
            dma((4,)),
            dma((2,)),
            dma((2, n_ctx)),
            dma((2, n_ctx)),
            dma((2,)),
            dma((2, blocks)),
            dma((2, blocks)),
            dma((count,)),
            dma((count,)),
            dma((2, blocks)),
            dma((2, 4)),
            dma((2, 4, n_ctx)),
            dma((2, 2)),
        ],
        compiler_params=pltpu.CompilerParams(
            collective_id=0, has_side_effects=True, vmem_limit_bytes=56 * 2**20
        ),
        name="hyena",
    )(
        seg_lengths, list_ids, streams, feat_taps, long_filter, upstream, score_dir[None, :],
        *[jnp.asarray(t, BF16) for t in TABLES],
    )
    return (d_streams, d_taps[:, :KF, :], d_filter)


def solution(mesh):
    placed = (
        P(None, ("groups", "ctx", "sub"), "fsdp"),
        P(None, None, "fsdp"),
        P("ctx", "fsdp"),
        P(("groups", "ctx", "sub"), "fsdp"),
        P("fsdp"),
        P("groups"),
        P("groups"),
    )
    sizes = (mesh.shape["ctx"], mesh.shape["fsdp"], mesh.shape["sub"])
    return jax.shard_map(
        functools.partial(local, sizes),
        mesh=mesh,
        in_specs=placed,
        out_specs=(
            P(None, ("groups", "ctx", "sub"), "fsdp"),
            P("groups", None, "fsdp"),
            P(("groups", "ctx"), "fsdp"),
        ),
        check_vma=False,
    )
```

```python
import functools

import jax
import jax.numpy as jnp
import numpy as np
from jax import lax
from jax.experimental import pallas as pl
from jax.experimental.pallas import tpu as pltpu
from jax.sharding import PartitionSpec as P

LH = 128
KF = 7
R = 128
F32 = jnp.float32
BF16 = jnp.bfloat16
MESH = pl.DeviceIdType.MESH

LEVELS = (64, 32, 16, 8, 4, 2, 1)
ROWS = 2 * LH + 128 * len(LEVELS)


def wave(m, positions):
    angle = np.pi * np.outer(2 * np.arange(m) + 1, positions) / (2 * m)
    return np.cos(angle), -np.sin(angle)


def tables():
    first, second, taps, out_first, out_second, out_taps = [], [], [], [], [], []
    for m in (LH,) + LEVELS:
        pairs = max(1, R // (2 * m))
        early, late, every = wave(m, np.arange(m)), wave(m, np.arange(m, 2 * m)), wave(m, np.arange(2 * m))
        span = min(2 * m, LH)
        for part in (0, 1):
            both = np.zeros((2, pairs * m, R))
            for g in range(pairs):
                rows = slice(g * m, (g + 1) * m)
                start = 2 * m * g
                both[0, rows, start : start + m] = early[part]
                both[1, rows, start + m if m < LH else 0 : start + 2 * m if m < LH else LH] = late[part]
            first.append(both[0])
            second.append(both[1])
            out_first.append(both[0].T / m)
            out_second.append(both[1].T / m)
            lag = np.zeros((m, LH))
            lag[:, 1:span] = every[part][:, 1:span]
            out_taps.append(np.tile(lag, (pairs, 1)).T / m)
            taps.append(np.tile(lag, (max(1, 16 // m), 1)))
    return (
        np.concatenate(first, 0), np.concatenate(second, 0), np.concatenate(taps, 0),
        np.concatenate(out_second, 1), np.concatenate(out_first, 1), np.concatenate(out_taps, 1),
    )


TABLES = [t.astype(np.float32) for t in tables()]
TAP_ROWS = TABLES[2].shape[0]


def starts(lens_ref):
    offsets, off = [], jnp.int32(0)
    for s in range(lens_ref.shape[0]):
        offsets.append(off)
        off = off + lens_ref[s]
    return offsets


def segment_of(offsets, position):
    seg = jnp.where(offsets[0] <= position, 0, -1)
    for off in offsets[1:]:
        seg = seg + jnp.where(off <= position, 1, 0)
    return seg


def age_of(offsets, position):
    start = jnp.zeros(position.shape, jnp.int32)
    for off in offsets:
        start = jnp.where(off <= position, off, start)
    return position - start


def down(rows):
    return lax.broadcasted_iota(jnp.int32, (rows, 1), 0)


def across(columns):
    return lax.broadcasted_iota(jnp.int32, (1, columns), 1)


def dot(a, b):
    return jnp.dot(a, b, preferred_element_type=F32)


def send(src, dst, sems, device):
    return pltpu.make_async_remote_copy(
        src_ref=src, dst_ref=dst, send_sem=sems[0], recv_sem=sems[1], device_id=device,
        device_id_type=MESH,
    )


def wide(row):
    return jnp.broadcast_to(row, (16, row.shape[1])).astype(BF16)


def scaled(tile, block):
    rows, width = block.shape
    return (block.reshape(rows // 16, 16, width) * tile[None]).reshape(rows, width)


def tap_parts(hat_ref, cols):
    parts, at = [], 0
    for m in (LH,) + LEVELS:
        rows, want = max(m, 16), max(64, m)
        pair = []
        for _ in range(2):
            piece = hat_ref[at : at + rows, cols]
            pair.append(piece if rows == want else jnp.concatenate([piece] * (want // rows), 0))
            at += rows
        parts.append(pair)
    return parts


def level_rows():
    spans, at = [], 0
    for m in (LH,) + LEVELS:
        half = max(64, m)
        spans.append((at, half))
        at += 2 * half
    return spans


def body(
    sizes, width,
    lens_ref, ids_ref, dir_ref, x_hbm, taps_hbm, fil_hbm, up_hbm, *refs,
):
    constants, refs = refs[:6], refs[6:]
    (
    dx_ref, dtaps_ref, out_ref,
    x_ref, taps_ref, all_ref, up_ref, upn_ref, feat_ref, z_ref, prev_ref, qn_ref, da_ref, dw_ref, w_ref,
    first_ref, second_ref, ftaps_ref, osecond_ref, ofirst_ref, otaps_ref, hd_ref, xs_ref, sum_ref, head_ref,
    hf_ref, hz_ref, own_first, prev_first, own_second, edge_second, next_second, inv_w, inv_d,
    fwd_ref, bwd_ref, shift_ref, stack_ref, prod_ref, proj_ref, coef_ref,
    part_ref, slots, fil_ref, dfil_ref, tap0_ref, tap1_ref, fil_a, fil_b, fil_c, fil_sum, tap0_a, tap0_b, tap0_c,
    tap1_a, tap1_b, tap1_c, tap_sum,
    load_sem, rim_sem, fil_sem, cross_sem, swap_sem, up_sem, z_sem, q_sem, sum_send, sum_recv, halo_sem,
    a_sem, b_sem, t_sem, c_sem,
    ) = refs
    n_ctx, n_fsdp, n_sub = sizes
    group, ctx = lax.axis_index("groups"), lax.axis_index("ctx")
    fsdp, sub = lax.axis_index("fsdp"), lax.axis_index("sub")
    chans = dir_ref.shape[1]
    half = chans // 2
    blocks = chans // width
    shard = fil_hbm.shape[0]
    segs = lens_ref.shape[0]
    line = ctx * 2 + sub
    base = line * R
    left = (group, (line - 1) // 2, fsdp, 1 - sub)
    right = (group, (line + 1) // 2, fsdp, 1 - sub)
    partner = (group, ctx, fsdp, 1 - sub)
    across_groups = (1 - group, ctx, fsdp, sub)
    has_left, has_right = line > 0, line < 2 * n_ctx - 1
    count = n_ctx * n_fsdp * n_sub
    me = (ctx * n_fsdp + fsdp) * n_sub + sub

    def where(r):
        peer = lax.rem(me + r, count)
        return (
            group, peer // (n_fsdp * n_sub), lax.rem(peer // n_sub, n_fsdp), lax.rem(peer, n_sub),
        )

    kept = pl.ds(pl.multiple_of(sub * half, half), half)
    quarter = pl.ds(pl.multiple_of((sub * 2 + group) * (half // 2), half // 2), half // 2)
    given = pl.ds(pl.multiple_of((1 - sub) * half, half), half)

    def columns(b):
        return pl.ds(pl.multiple_of(b * width, width), width)

    barrier = pltpu.get_barrier_semaphore()

    def greet(r, carry):
        pl.semaphore_signal(barrier, inc=1, device_id=where(r), device_id_type=MESH)
        return carry

    pl.semaphore_signal(barrier, inc=1, device_id=across_groups, device_id_type=MESH)
    lax.fori_loop(1, count, greet, 0)
    held = (first_ref, second_ref, ftaps_ref, osecond_ref, ofirst_ref, otaps_ref)
    loads = [
        pltpu.make_async_copy(source, target, load_sem.at[4 + n])
        for n, (source, target) in enumerate(zip(constants, held))
    ] + [
        pltpu.make_async_copy(x_hbm, x_ref.at[:, pl.ds(16, R), :], load_sem.at[0]),
        pltpu.make_async_copy(taps_hbm, taps_ref, load_sem.at[1]),
        pltpu.make_async_copy(fil_hbm, all_ref.at[ctx], load_sem.at[2]),
        pltpu.make_async_copy(up_hbm, up_ref, load_sem.at[3]),
    ]
    for load in loads:
        load.start()

    def rim_copy():
        return send(
            x_hbm.at[:, pl.ds(R - 16, 16), :], x_ref.at[:, pl.ds(0, 16), :],
            (rim_sem.at[0], rim_sem.at[1]), right,
        )

    def up_copy():
        return send(up_hbm, upn_ref, (up_sem.at[0], up_sem.at[1]), left)

    def fil_copy(r):
        return send(
            fil_hbm.at[:, quarter], all_ref.at[ctx, :, quarter], (fil_sem.at[0, r], fil_sem.at[1, r]),
            (group, lax.rem(ctx + r, n_ctx), fsdp, sub),
        )

    def cross_copy(r):
        held = lax.rem(ctx - r + n_ctx, n_ctx)
        return send(
            all_ref.at[held, :, quarter], all_ref.at[held, :, quarter],
            (cross_sem.at[0, r], cross_sem.at[1, r]), across_groups,
        )

    def swap_copy(r):
        held = lax.rem(ctx - r + n_ctx, n_ctx)
        return send(
            all_ref.at[held, :, kept], all_ref.at[held, :, kept],
            (swap_sem.at[0, r], swap_sem.at[1, r]), partner,
        )

    def z_copy(b):
        cols = columns(b)
        return send(
            z_ref.at[pl.ds(16, R - 16), cols], prev_ref.at[pl.ds(16, R - 16), cols],
            (z_sem.at[0, b], z_sem.at[1, b]), right,
        )

    def z_head_copy():
        return send(
            z_ref.at[pl.ds(0, 16), :], prev_ref.at[pl.ds(0, 16), :],
            (z_sem.at[0, blocks], z_sem.at[1, blocks]), right,
        )

    def q_copy(b):
        cols = columns(b)
        return send(
            feat_ref.at[0, :, cols], qn_ref.at[:, cols], (q_sem.at[0, b], q_sem.at[1, b]), left
        )

    def halo_copy(b):
        cols = columns(b)
        return send(
            da_ref.at[:, pl.ds(0, 16), cols], da_ref.at[:, pl.ds(R, 16), cols],
            (halo_sem.at[0, b], halo_sem.at[1, b]), left,
        )

    offsets = starts(lens_ref)
    age_down = age_of(offsets, base + down(R))
    age_over = age_of(offsets, base + across(R))
    gap = across(R) - down(R)
    lane = across(R)
    rim_gap = jnp.where(lane < 16 * KF, lane % 16 - 16 + lane // 16, 4 * R) - down(R)
    halo_age = age_of(offsets, base + R + lane % 16)
    halo_gap = jnp.where(lane < 16 * KF, lane % 16 + R - lane // 16, 4 * R) - down(R)
    for j in range(KF):
        span = slice(j * R, (j + 1) * R)
        fwd_ref[:, span] = jnp.where((gap == -j) & (age_down >= j), 1.0, 0.0).astype(BF16)
        bwd_ref[:, span] = jnp.where((gap == j) & (age_over >= j), 1.0, 0.0).astype(BF16)
        wide_gap = across(R + 16) - down(R) - 16
        shift_ref[span, :] = jnp.where((wide_gap == -j) & (age_down >= j), 1.0, 0.0).astype(BF16)
    sum_ref[...] = jnp.where(across(KF * R) // R == down(16), 1.0, 0.0).astype(BF16)
    span = slice(KF * R, (KF + 1) * R)
    fwd_ref[:, span] = jnp.where((rim_gap == 0) & (age_down >= lane // 16), 1.0, 0.0).astype(BF16)
    bwd_ref[:, span] = jnp.where((halo_gap == 0) & (halo_age >= lane // 16), 1.0, 0.0).astype(BF16)
    stack_ref[:, KF * (R + 16) :, :] = jnp.zeros((3, R - 16 * KF, width), BF16)

    pl.semaphore_wait(barrier, count)

    @pl.when(has_right)
    def _():
        rim_copy().start()

    for r in range(1, n_ctx):
        fil_copy(r).start()

    @pl.when(has_left)
    def _():
        up_copy().start()

    @pl.when(jnp.logical_not(has_left))
    def _():
        x_ref[:, 0:16, :] = jnp.zeros((3, 16, chans), BF16)
        prev_ref[...] = jnp.zeros(prev_ref.shape, BF16)

    @pl.when(jnp.logical_not(has_right))
    def _():
        upn_ref[...] = jnp.zeros(upn_ref.shape, BF16)
        qn_ref[...] = jnp.zeros(qn_ref.shape, BF16)
        da_ref[:, R:, :] = jnp.zeros((3, 16, chans), BF16)

    for load in loads[: len(held)]:
        load.wait()

    def kept_rows(table, mask):
        return jnp.where(mask, table.astype(F32), 0.0).astype(BF16)

    seg_down = segment_of(offsets, base + down(R))
    seg_over = segment_of(offsets, base + lane)
    seg_here, seg_next = segment_of(offsets, base + down(1)), segment_of(offsets, base + R + down(1))
    prev_mask = segment_of(offsets, base - R + lane) == seg_here
    next_mask = segment_of(offsets, base + R + lane) == seg_next
    prev_first[...] = kept_rows(first_ref[: 2 * LH], prev_mask)
    edge_second[...] = kept_rows(second_ref[: 2 * LH], seg_over == seg_here)
    next_second[...] = kept_rows(second_ref[: 2 * LH], next_mask)
    inv_w[:, : 2 * LH] = kept_rows(osecond_ref[:, : 2 * LH], seg_down == seg_here)
    inv_d[:, : 2 * LH] = kept_rows(ofirst_ref[:, : 2 * LH], seg_down == seg_next)
    for i, m in enumerate(LEVELS):
        at, to = 2 * LH + 128 * i, 128 * i
        mask = segment_of(offsets, base + lane // (2 * m) * (2 * m) + m) == seg_over
        own_first[to : to + 128] = kept_rows(first_ref[at : at + 128], mask)
        own_second[to : to + 128] = kept_rows(second_ref[at : at + 128], mask)
        mask = segment_of(offsets, base + down(R) // (2 * m) * (2 * m) + m) == seg_down
        inv_w[:, at : at + 128] = kept_rows(osecond_ref[:, at : at + 128], mask)
        inv_d[:, at : at + 128] = kept_rows(ofirst_ref[:, at : at + 128], mask)

    for load in loads[len(held):]:
        load.wait()

    def stack_near(i, source, near, cols):
        for j in range(KF):
            tile = wide(taps_ref[i, j : j + 1, cols])
            stack_ref[i, j * R : (j + 1) * R, :] = scaled(tile, source[i, near, cols])

    def stack_far(i, source, far, cols):
        for j in range(KF):
            tile = wide(taps_ref[i, j : j + 1, cols])
            at = KF * R + 16 * j
            stack_ref[i, at : at + 16, :] = scaled(tile, source[i, far, cols])

    def feat_block(b, carry):
        cols = columns(b)
        feats = [None] * 3
        for i in (1, 2, 0):
            stack_near(i, x_ref, slice(16, 16 + R), cols)
            total = dot(fwd_ref[:, : KF * R], stack_ref[i, : KF * R, :])
            head_ref[i, :, cols] = total[:16]
            feats[i] = total[16:].astype(BF16)
            feat_ref[i, 16:, cols] = feats[i]
        z_ref[16:, cols] = (feats[1].astype(F32) * feats[2].astype(F32)).astype(BF16)

        @pl.when(has_right)
        def _():
            z_copy(b).start()

        return carry

    lax.fori_loop(0, blocks, feat_block, 0)

    @pl.when(has_left)
    def _():
        rim_copy().wait_recv()

    def head_block(b, carry):
        cols = columns(b)
        feats = [None] * 3
        for i in range(3):
            stack_far(i, x_ref, slice(0, 16), cols)
            feats[i] = (
                head_ref[i, :, cols] + dot(fwd_ref[0:16, KF * R :], stack_ref[i, KF * R :, :])
            ).astype(BF16)
            feat_ref[i, 0:16, cols] = feats[i]
        z_ref[0:16, cols] = (feats[1].astype(F32) * feats[2].astype(F32)).astype(BF16)

        @pl.when(has_left)
        def _():
            q_copy(b).start()

        return carry

    lax.fori_loop(0, blocks, head_block, 0)

    @pl.when(has_right)
    def _():
        z_head_copy().start()

    for r in range(1, n_ctx):
        fil_copy(r).wait_recv()
        cross_copy(r).start()

    def own_hat_block(b, carry):
        cols = columns(b)
        hz_ref[2 * LH :, cols] = dot(own_first[...], z_ref[:, cols]).astype(BF16)
        return carry

    lax.fori_loop(0, blocks, own_hat_block, 0)

    for r in range(1, n_ctx):
        cross_copy(r).wait_recv()
        swap_copy(r).start()
    for r in range(1, n_ctx):
        swap_copy(r).wait_recv()

    def fil_block(b, carry):
        cols = columns(b)
        taps = all_ref[:, :, cols].astype(F32).reshape(LH, width)
        fil_ref[0:8, cols] = taps[0:8]
        hf_ref[:, cols] = dot(ftaps_ref[...], taps.astype(BF16)).astype(BF16)
        return carry

    lax.fori_loop(0, blocks, fil_block, 0)

    proj_ref[...] = jnp.zeros(proj_ref.shape, F32)

    @pl.when(has_left)
    def _():
        z_head_copy().wait_recv()

    def mix_block(b, carry):
        cols = columns(b)

        @pl.when(has_left)
        def _():
            z_copy(b).wait_recv()

        hz_ref[: 2 * LH, cols] = dot(prev_first[...], prev_ref[:, cols]).astype(BF16)
        for (at, n), (f_re, f_im) in zip(level_rows(), tap_parts(hf_ref, cols)):
            z_re, z_im = hz_ref[at : at + n, cols], hz_ref[at + n : at + 2 * n, cols]
            prod_ref[at : at + n, :] = f_re * z_re - f_im * z_im
            prod_ref[at + n : at + 2 * n, :] = f_re * z_im + f_im * z_re
        w = dot(inv_w[...], prod_ref[...]) + fil_ref[0:1, cols] * z_ref[:, cols].astype(F32)
        w_ref[:, cols] = w
        weighted = feat_ref[0, :, cols].astype(F32) * w * dir_ref[:, cols]
        part = weighted[:, 0:128]
        for c in range(1, width // 128):
            part = part + weighted[:, c * 128 : (c + 1) * 128]
        proj_ref[...] += part
        return carry

    lax.fori_loop(0, blocks, mix_block, 0)

    for s in range(segs):
        part_ref[s : s + 1, :] = jnp.sum(
            jnp.where(seg_down == s, proj_ref[...], 0.0), axis=0, keepdims=True
        )

    def sum_copy(r):
        return send(part_ref, slots.at[r], (sum_send.at[r], sum_recv.at[r]), where(r))

    def begin(r, carry):
        sum_copy(r).start()
        return carry

    def end(r, carry):
        sum_copy(r).wait()
        return carry

    lax.fori_loop(1, count, begin, 0)

    def shift_block(b, carry):
        cols = columns(b)
        for i in range(3):
            xs_ref[i, :, cols] = dot(shift_ref[...], x_ref[i, :, cols]).astype(BF16)
        return carry

    ids, id_row = jnp.zeros((segs, 1), jnp.int32), jnp.zeros((1, segs), jnp.int32)
    lengths = jnp.zeros((segs, 1), jnp.int32)
    for s in range(segs):
        ids = jnp.where(down(segs) == s, ids_ref[s], ids)
        id_row = jnp.where(across(segs) == s, ids_ref[s], id_row)
        lengths = jnp.where(down(segs) == s, lens_ref[s], lengths)
    lengths = lengths.astype(F32)
    same = down(segs) == across(segs)
    mates = jnp.where(ids == id_row, 1.0, 0.0)
    mate_count = jnp.sum(mates, axis=1, keepdims=True)
    hot = segment_of(offsets, base + down(2 * R)) == across(segs)
    lax.fori_loop(0, blocks, shift_block, 0)
    slots[0] = part_ref[...]
    lax.fori_loop(1, count, end, 0)

    def add_slot(i, total):
        return total + slots[lax.rem(me - i + count, count)]

    summed = lax.fori_loop(0, count, add_slot, jnp.zeros(part_ref.shape, F32))
    scores = jnp.sum(summed, axis=1, keepdims=True) / lengths
    score_row = jnp.sum(jnp.where(same, scores, 0.0), axis=0, keepdims=True)
    means = jnp.sum(mates * score_row, axis=1, keepdims=True) / mate_count
    coef = (scores - means) / lengths
    coef_row = jnp.sum(jnp.where(same, coef, 0.0), axis=0, keepdims=True)
    coef_ref[...] = jnp.sum(jnp.where(hot, coef_row, 0.0), axis=1, keepdims=True)

    def own_block(b, carry):
        cols = columns(b)
        d_out = up_ref[:, cols].astype(F32) + coef_ref[0:R, :] * dir_ref[:, cols]
        da_ref[0, 0:R, cols] = (d_out * w_ref[:, cols]).astype(BF16)
        dw = (d_out * feat_ref[0, :, cols].astype(F32)).astype(BF16)
        dw_ref[:, cols] = dw
        edge = dot(edge_second[...], dw).astype(BF16)
        hd_ref[:, cols] = dot(own_second[...], dw).astype(BF16)
        for at, n in level_rows():
            if at == 0:
                d_re, d_im = edge[:n], edge[n:]
            else:
                to = at - 2 * LH
                d_re, d_im = hd_ref[to : to + n, cols], hd_ref[to + n : to + 2 * n, cols]
            z_re, z_im = hz_ref[at : at + n, cols], hz_ref[at + n : at + 2 * n, cols]
            prod_ref[at : at + n, :] = z_re * d_re + z_im * d_im
            prod_ref[at + n : at + 2 * n, :] = z_re * d_im - z_im * d_re
        whole = jnp.sum(dw.astype(F32) * z_ref[:, cols].astype(F32), axis=0, keepdims=True)
        dfil = dot(otaps_ref[...], prod_ref[...]) + jnp.where(down(LH) == 0, whole, 0.0)
        dfil_ref[:, :, cols] = dfil.reshape(n_ctx, shard, width).astype(BF16)
        return carry

    def grad_block(b, carry):
        cols = columns(b)

        @pl.when(has_right)
        def _():
            q_copy(b).wait_recv()

        d_next = upn_ref[:, cols].astype(F32) + coef_ref[R:, :] * dir_ref[:, cols]
        dw_next = (d_next * qn_ref[:, cols].astype(F32)).astype(BF16)
        after = dot(next_second[...], dw_next).astype(BF16)
        for (at, n), (f_re, f_im) in zip(level_rows(), tap_parts(hf_ref, cols)):
            if at == 0:
                d_re, d_im = after[:n], after[n:]
            else:
                to = at - 2 * LH
                d_re, d_im = hd_ref[to : to + n, cols], hd_ref[to + n : to + 2 * n, cols]
            prod_ref[at : at + n, :] = f_re * d_re + f_im * d_im
            prod_ref[at + n : at + 2 * n, :] = f_re * d_im - f_im * d_re
        dz = dot(inv_d[...], prod_ref[...]) + fil_ref[0:1, cols] * dw_ref[:, cols].astype(F32)
        da_ref[1, 0:R, cols] = (dz * feat_ref[2, :, cols].astype(F32)).astype(BF16)
        da_ref[2, 0:R, cols] = (dz * feat_ref[1, :, cols].astype(F32)).astype(BF16)

        @pl.when(has_left)
        def _():
            halo_copy(b).start()

        return carry

    phases = n_ctx.bit_length() - 1

    def peer(p):
        other = ctx + (1 - 2 * lax.rem(ctx // 2**p, 2)) * 2**p
        return other, (group, other, fsdp, sub)

    def fil_swap():
        return send(dfil_ref.at[:, :, given], fil_a, (a_sem.at[0, 0], a_sem.at[1, 0]), partner)

    def fil_step(p, k):
        slot = n_ctx - (n_ctx >> p) + k
        other, device = peer(p)
        wanted = lax.rem(other, 2 ** (p + 1)) + k * 2 ** (p + 1)
        return send(fil_c.at[wanted], fil_b.at[slot], (b_sem.at[0, slot], b_sem.at[1, slot]), device)

    def fil_begin(p):
        for k in range(n_ctx >> (p + 1)):
            fil_step(p, k).start()

    def fil_end(p):
        totals = []
        for k in range(n_ctx >> (p + 1)):
            fil_step(p, k).wait()
            mine = lax.rem(ctx, 2 ** (p + 1)) + k * 2 ** (p + 1)
            slot = n_ctx - (n_ctx >> p) + k
            totals.append(fil_c[mine].astype(F32) + fil_b[slot].astype(F32))
            if p < phases - 1:
                fil_c[mine] = totals[-1].astype(BF16)
        return totals[0]

    tap_sets = ((tap0_ref, tap0_a, tap0_b, tap0_c), (tap1_ref, tap1_a, tap1_b, tap1_c))

    def tap_swap(c):
        own, got, _, _ = tap_sets[c]
        return send(own.at[:, :, given], got, (a_sem.at[0, 1 + c], a_sem.at[1, 1 + c]), partner)

    def tap_step(c, p):
        _, _, slots_of, running = tap_sets[c]
        return send(running, slots_of.at[p], (t_sem.at[0, c, p], t_sem.at[1, c, p]), peer(p)[1])

    def tap_first(c):
        tap_swap(c).wait()
        own, got, _, running = tap_sets[c]
        running[...] = (own[:, :, kept].astype(F32) + got[...].astype(F32)).astype(BF16)
        tap_step(c, 0).start()

    def tap_end(c, p):
        _, _, slots_of, running = tap_sets[c]
        tap_step(c, p).wait()
        total = running[...].astype(F32) + slots_of[p].astype(F32)
        if p < phases - 1:
            running[...] = total.astype(BF16)
        return total

    last = [
        send(fil_sum, out_ref.at[:, kept], (c_sem.at[0, 0], c_sem.at[1, 0]), partner),
        send(tap_sum, dtaps_ref.at[:, :, kept], (c_sem.at[0, 1], c_sem.at[1, 1]), partner),
    ]

    def tap_sums(i):
        def block(b, carry):
            cols = columns(b)
            own = da_ref[i, 0:R, cols]
            for j in range(KF):
                span = slice(j * R, (j + 1) * R)
                stack_ref[i, span, :] = own * xs_ref[i, span, cols]
            sums = dot(sum_ref[...], stack_ref[i, : KF * R, :])[0:8].astype(BF16)
            if i == 0:
                tap0_ref[0, :, cols] = sums
            else:
                tap1_ref[i - 1, :, cols] = sums
            return carry

        lax.fori_loop(0, blocks, block, 0)

    def stream(i):
        def block(b, carry):
            cols = columns(b)
            stack_near(i, da_ref, slice(0, R), cols)
            stack_far(i, da_ref, slice(R, R + 16), cols)
            dx_ref[i, :, cols] = dot(bwd_ref[...], stack_ref[i]).astype(BF16)
            return carry

        lax.fori_loop(0, blocks, block, 0)

    def relay(c):
        first[c].wait()
        if c == 0:
            fil_c[...] = (dfil_ref[:, :, kept].astype(F32) + fil_a[...].astype(F32)).astype(BF16)
        else:
            i = c - 1
            tap_c[i] = (tap_ref[i, :, kept].astype(F32) + tap_a[i].astype(F32)).astype(BF16)
        for r in range(1, n_ctx):
            second(c, r).start()

    per_half = blocks // 2
    lax.fori_loop((1 - sub) * per_half, (2 - sub) * per_half, own_block, 0)
    fil_swap().start()
    lax.fori_loop(sub * per_half, (1 + sub) * per_half, own_block, 0)
    tap_sums(0)
    tap_swap(0).start()
    fil_swap().wait()
    fil_c[...] = (dfil_ref[:, :, kept].astype(F32) + fil_a[...].astype(F32)).astype(BF16)
    fil_begin(0)

    @pl.when(has_right)
    def _():
        up_copy().wait_recv()

    lax.fori_loop(0, per_half, grad_block, 0)
    tap_first(0)
    lax.fori_loop(per_half, blocks, grad_block, 0)
    tap_sums(1)
    tap_sums(2)
    tap_swap(1).start()
    for p in range(phases - 1):
        fil_end(p)
        fil_begin(p + 1)
    for p in range(phases - 1):
        tap_end(0, p)
        tap_step(0, p + 1).start()

    @pl.when(has_right)
    def _():
        for b in range(blocks):
            halo_copy(b).wait_recv()

    tap_first(1)
    stream(0)
    for p in range(phases - 1):
        tap_end(1, p)
        tap_step(1, p + 1).start()
    stream(1)
    total = fil_end(phases - 1)
    fil_sum[...] = total
    out_ref[:, kept] = total
    last[0].start()
    stream(2)
    taps_total = tap_end(0, phases - 1)[:, :KF]
    tap_sum[0:1] = taps_total
    dtaps_ref[0:1, :, kept] = taps_total
    taps_total = tap_end(1, phases - 1)[:, :KF]
    tap_sum[1:3] = taps_total
    dtaps_ref[1:3, :, kept] = taps_total
    last[1].start()

    @pl.when(has_left)
    def _():
        up_copy().wait_send()
        for b in range(blocks):
            q_copy(b).wait_send()
            halo_copy(b).wait_send()

    @pl.when(has_right)
    def _():
        rim_copy().wait_send()
        z_head_copy().wait_send()
        for b in range(blocks):
            z_copy(b).wait_send()

    for r in range(1, n_ctx):
        fil_copy(r).wait_send()
        cross_copy(r).wait_send()
        swap_copy(r).wait_send()
    last[0].wait()
    last[1].wait()


def store(dx_ref, dtaps_ref, dfil_ref, dx_out, dtaps_out, dfil_out, sems):
    copies = [
        pltpu.make_async_copy(dx_ref, dx_out, sems.at[0]),
        pltpu.make_async_copy(dtaps_ref, dtaps_out, sems.at[1]),
        pltpu.make_async_copy(dfil_ref, dfil_out, sems.at[2]),
    ]
    for copy in copies:
        copy.start()
    for copy in copies:
        copy.wait()


def local(sizes, streams, feat_taps, long_filter, upstream, score_dir, seg_lengths, list_ids):
    rows, chans = streams.shape[1:]
    assert rows == R
    width = min(1024, chans // 2)
    blocks = chans // width
    half = chans // 2
    n_ctx = sizes[0]
    count = sizes[0] * sizes[1] * sizes[2]
    shard = long_filter.shape[0]
    segs = seg_lengths.shape[0]
    vmem = pl.BlockSpec(memory_space=pltpu.VMEM)
    smem = pl.BlockSpec(memory_space=pltpu.SMEM)
    hbm = pl.BlockSpec(memory_space=pl.ANY)
    dma = pltpu.SemaphoreType.DMA
    own = ROWS - 2 * LH
    phases = n_ctx.bit_length() - 1
    assert n_ctx == 2**phases
    d_streams, d_taps, d_filter = pl.pallas_call(
        functools.partial(body, sizes, width),
        in_specs=[smem, smem, vmem] + [hbm] * 10,
        out_specs=[vmem] * 3,
        out_shape=[
            pltpu.VMEM((3, rows, chans), BF16),
            pltpu.VMEM((3, KF, chans), F32),
            pltpu.VMEM((shard, chans), F32),
        ],
        scratch_shapes=[
            pltpu.VMEM((3, R + 16, chans), BF16),
            pltpu.VMEM((3, KF, chans), F32),
            pltpu.VMEM((n_ctx, shard, chans), BF16),
            pltpu.VMEM((R, chans), BF16),
            pltpu.VMEM((R, chans), BF16),
            pltpu.VMEM((3, R, chans), BF16),
            pltpu.VMEM((R, chans), BF16),
            pltpu.VMEM((R, chans), BF16),
            pltpu.VMEM((R, chans), BF16),
            pltpu.VMEM((3, R + 16, chans), BF16),
            pltpu.VMEM((R, chans), BF16),
            pltpu.VMEM((R, chans), F32),
            *[pltpu.VMEM(t.shape, BF16) for t in TABLES],
            pltpu.VMEM((own, chans), BF16),
            pltpu.VMEM((3, KF * R, chans), BF16),
            pltpu.VMEM((16, KF * R), BF16),
            pltpu.VMEM((3, 16, chans), F32),
            pltpu.VMEM((TAP_ROWS, chans), BF16),
            pltpu.VMEM((ROWS, chans), BF16),
            pltpu.VMEM((own, R), BF16),
            pltpu.VMEM((2 * LH, R), BF16),
            pltpu.VMEM((own, R), BF16),
            pltpu.VMEM((2 * LH, R), BF16),
            pltpu.VMEM((2 * LH, R), BF16),
            pltpu.VMEM((R, ROWS), BF16),
            pltpu.VMEM((R, ROWS), BF16),
            pltpu.VMEM((R, (KF + 1) * R), BF16),
            pltpu.VMEM((R, (KF + 1) * R), BF16),
            pltpu.VMEM((KF * R, R + 16), BF16),
            pltpu.VMEM((3, (KF + 1) * R, width), BF16),
            pltpu.VMEM((ROWS, width), BF16),
            pltpu.VMEM((R, 128), F32),
            pltpu.VMEM((2 * R, 1), F32),
            pltpu.VMEM((segs, 128), F32),
            pltpu.VMEM((count, segs, 128), F32),
            pltpu.VMEM((8, chans), F32),
            pltpu.VMEM((n_ctx, shard, chans), BF16),
            pltpu.VMEM((1, 8, chans), BF16),
            pltpu.VMEM((2, 8, chans), BF16),
            pltpu.VMEM((n_ctx, shard, half), BF16),
            pltpu.VMEM((n_ctx, shard, half), BF16),
            pltpu.VMEM((n_ctx, shard, half), BF16),
            pltpu.VMEM((shard, half), F32),
            pltpu.VMEM((1, 8, half), BF16),
            pltpu.VMEM((phases, 1, 8, half), BF16),
            pltpu.VMEM((1, 8, half), BF16),
            pltpu.VMEM((2, 8, half), BF16),
            pltpu.VMEM((phases, 2, 8, half), BF16),
            pltpu.VMEM((2, 8, half), BF16),
            pltpu.VMEM((3, KF, half), F32),
            dma((4 + len(TABLES),)),
            dma((2,)),
            dma((2, n_ctx)),
            dma((2, n_ctx)),
            dma((2, n_ctx)),
            dma((2,)),
            dma((2, blocks + 1)),
            dma((2, blocks)),
            dma((count,)),
            dma((count,)),
            dma((2, blocks)),
            dma((2, 3)),
            dma((2, n_ctx)),
            dma((2, 2, phases)),
            dma((2, 2)),
        ],
        compiler_params=pltpu.CompilerParams(
            collective_id=0, has_side_effects=True, vmem_limit_bytes=54 * 2**20
        ),
        name="hyena",
    )(
        seg_lengths, list_ids, score_dir[None, :], streams, feat_taps, long_filter, upstream,
        *[jnp.asarray(t, BF16) for t in TABLES],
    )
    return pl.pallas_call(
        store,
        in_specs=[hbm] * 3,
        out_specs=[hbm] * 3,
        out_shape=[
            jax.ShapeDtypeStruct((3, rows, chans), BF16),
            jax.ShapeDtypeStruct((3, KF, chans), F32),
            jax.ShapeDtypeStruct((shard, chans), F32),
        ],
        scratch_shapes=[dma((3,))],
        compiler_params=pltpu.CompilerParams(vmem_limit_bytes=2**20),
        name="store",
    )(d_streams, d_taps, d_filter)


def solution(mesh):
    placed = (
        P(None, ("groups", "ctx", "sub"), "fsdp"),
        P(None, None, "fsdp"),
        P("ctx", "fsdp"),
        P(("groups", "ctx", "sub"), "fsdp"),
        P("fsdp"),
        P("groups"),
        P("groups"),
    )
    sizes = (mesh.shape["ctx"], mesh.shape["fsdp"], mesh.shape["sub"])
    return jax.shard_map(
        functools.partial(local, sizes),
        mesh=mesh,
        in_specs=placed,
        out_specs=(
            P(None, ("groups", "ctx", "sub"), "fsdp"),
            P("groups", None, "fsdp"),
            P(("groups", "ctx"), "fsdp"),
        ),
        check_vma=False,
    )
```

```python
import functools

import jax
import jax.numpy as jnp
import numpy as np
from jax import lax
from jax.experimental import pallas as pl
from jax.experimental.pallas import tpu as pltpu
from jax.sharding import PartitionSpec as P

LH = 128
KF = 7
R = 128
F32 = jnp.float32
BF16 = jnp.bfloat16
MESH = pl.DeviceIdType.MESH

LEVELS = (64, 32, 16, 8, 4, 2, 1)
ROWS = 2 * LH + 128 * len(LEVELS)


def wave(m, positions):
    angle = np.pi * np.outer(2 * np.arange(m) + 1, positions) / (2 * m)
    return np.cos(angle), -np.sin(angle)


def tables():
    first, second, taps, out_first, out_second, out_taps = [], [], [], [], [], []
    for m in (LH,) + LEVELS:
        pairs = max(1, R // (2 * m))
        early, late, every = wave(m, np.arange(m)), wave(m, np.arange(m, 2 * m)), wave(m, np.arange(2 * m))
        span = min(2 * m, LH)
        for part in (0, 1):
            both = np.zeros((2, pairs * m, R))
            for g in range(pairs):
                rows = slice(g * m, (g + 1) * m)
                start = 2 * m * g
                both[0, rows, start : start + m] = early[part]
                both[1, rows, start + m if m < LH else 0 : start + 2 * m if m < LH else LH] = late[part]
            first.append(both[0])
            second.append(both[1])
            out_first.append(both[0].T / m)
            out_second.append(both[1].T / m)
            lag = np.zeros((m, LH))
            lag[:, 1:span] = every[part][:, 1:span]
            out_taps.append(np.tile(lag, (pairs, 1)).T / m)
            taps.append(np.tile(lag, (max(1, 16 // m), 1)))
    return (
        np.concatenate(first, 0), np.concatenate(second, 0), np.concatenate(taps, 0),
        np.concatenate(out_second, 1), np.concatenate(out_first, 1), np.concatenate(out_taps, 1),
    )


TABLES = [t.astype(np.float32) for t in tables()]
TAP_ROWS = TABLES[2].shape[0]


def starts(lens_ref):
    offsets, off = [], jnp.int32(0)
    for s in range(lens_ref.shape[0]):
        offsets.append(off)
        off = off + lens_ref[s]
    return offsets


def segment_of(offsets, position):
    seg = jnp.where(offsets[0] <= position, 0, -1)
    for off in offsets[1:]:
        seg = seg + jnp.where(off <= position, 1, 0)
    return seg


def age_of(offsets, position):
    start = jnp.zeros(position.shape, jnp.int32)
    for off in offsets:
        start = jnp.where(off <= position, off, start)
    return position - start


def down(rows):
    return lax.broadcasted_iota(jnp.int32, (rows, 1), 0)


def across(columns):
    return lax.broadcasted_iota(jnp.int32, (1, columns), 1)


def dot(a, b):
    return jnp.dot(a, b, preferred_element_type=F32)


def send(src, dst, sems, device):
    return pltpu.make_async_remote_copy(
        src_ref=src, dst_ref=dst, send_sem=sems[0], recv_sem=sems[1], device_id=device,
        device_id_type=MESH,
    )


def wide(row):
    return jnp.broadcast_to(row, (16, row.shape[1])).astype(BF16)


def scaled(tile, block):
    rows, width = block.shape
    return (block.reshape(rows // 16, 16, width) * tile[None]).reshape(rows, width)


def packed(parts):
    wide_parts = [part.astype(F32) for part in parts] + [jnp.zeros(parts[0].shape, F32)]
    return [jnp.concatenate(wide_parts[n : n + 2], 0).astype(BF16) for n in (0, 2)]


def unpacked(tiles):
    both, one = tiles[0].astype(F32), tiles[1].astype(F32)
    return [both[0:8], both[8:16], one[0:8]]


def tap_parts(hat_ref, cols):
    parts, at = [], 0
    for m in (LH,) + LEVELS:
        rows, want = max(m, 16), max(64, m)
        pair = []
        for _ in range(2):
            piece = hat_ref[at : at + rows, cols]
            pair.append(piece if rows == want else jnp.concatenate([piece] * (want // rows), 0))
            at += rows
        parts.append(pair)
    return parts


def level_rows():
    spans, at = [], 0
    for m in (LH,) + LEVELS:
        half = max(64, m)
        spans.append((at, half))
        at += 2 * half
    return spans


def body(
    sizes, width,
    lens_ref, ids_ref, dir_ref, x_hbm, taps_hbm, fil_hbm, up_hbm, *refs,
):
    constants, refs = refs[:6], refs[6:]
    (
    dx_ref, dtaps_ref, out_ref,
    x_ref, taps_ref, all_ref, up_ref, upn_ref, feat_ref, z_ref, prev_ref, qn_ref, da_ref, dw_ref, w_ref,
    first_ref, second_ref, ftaps_ref, osecond_ref, ofirst_ref, otaps_ref, hd_ref, xs_ref, sum_ref, head_ref, rim_out, rim_in, halo_out, halo_in,
    hf_ref, hz_ref, own_first, prev_first, own_second, edge_second, next_second, inv_w, inv_d,
    fwd_ref, bwd_ref, shift_ref, stack_ref, prod_ref, proj_ref, coef_ref,
    part_ref, slots, fil_ref, dfil_ref, tap0_ref, tap1_ref, fil_a, fil_b, fil_c, fil_sum, tap0_a, tap0_b, tap0_c,
    tap1_a, tap1_b, tap1_c, tap_sum,
    load_sem, rim_sem, fil_sem, cross_sem, swap_sem, up_sem, z_sem, q_sem, sum_send, sum_recv, halo_sem,
    a_sem, b_sem, t_sem, c_sem,
    ) = refs
    n_ctx, n_fsdp, n_sub = sizes
    group, ctx = lax.axis_index("groups"), lax.axis_index("ctx")
    fsdp, sub = lax.axis_index("fsdp"), lax.axis_index("sub")
    chans = dir_ref.shape[1]
    half = chans // 2
    blocks = chans // width
    shard = fil_hbm.shape[0]
    segs = lens_ref.shape[0]
    line = ctx * 2 + sub
    base = line * R
    left = (group, (line - 1) // 2, fsdp, 1 - sub)
    right = (group, (line + 1) // 2, fsdp, 1 - sub)
    partner = (group, ctx, fsdp, 1 - sub)
    across_groups = (1 - group, ctx, fsdp, sub)
    has_left, has_right = line > 0, line < 2 * n_ctx - 1
    count = n_ctx * n_fsdp * n_sub

    def where(r):
        return (
            group,
            lax.rem(ctx + r // (n_fsdp * n_sub), n_ctx),
            lax.rem(fsdp + r // n_sub % n_fsdp, n_fsdp),
            lax.rem(sub + r % n_sub, n_sub),
        )

    def each_peer(step):
        if count <= 32:
            for r in range(1, count):
                step(r)
        else:
            lax.fori_loop(1, count, lambda r, carry: (step(r), carry)[1], 0)

    kept = pl.ds(pl.multiple_of(sub * half, half), half)
    quarter = pl.ds(pl.multiple_of((sub * 2 + group) * (half // 2), half // 2), half // 2)
    given = pl.ds(pl.multiple_of((1 - sub) * half, half), half)

    def columns(b):
        return pl.ds(pl.multiple_of(b * width, width), width)

    barrier = pltpu.get_barrier_semaphore()

    def greet(r):
        pl.semaphore_signal(barrier, inc=1, device_id=where(r), device_id_type=MESH)

    pl.semaphore_signal(barrier, inc=1, device_id=across_groups, device_id_type=MESH)
    each_peer(greet)
    held = (first_ref, second_ref, ftaps_ref, osecond_ref, ofirst_ref, otaps_ref)
    loads = [
        pltpu.make_async_copy(x_hbm, x_ref.at[:, pl.ds(16, R), :], load_sem.at[0]),
        pltpu.make_async_copy(taps_hbm, taps_ref, load_sem.at[1]),
        pltpu.make_async_copy(fil_hbm, all_ref.at[ctx], load_sem.at[2]),
        pltpu.make_async_copy(up_hbm, up_ref, load_sem.at[3]),
    ] + [
        pltpu.make_async_copy(source, target, load_sem.at[4 + n])
        for n, (source, target) in enumerate(zip(constants, held))
    ]
    for load in loads:
        load.start()

    def rim_copy():
        return send(
            rim_out, rim_in, (rim_sem.at[0], rim_sem.at[1]), right,
        )

    def up_copy():
        return send(up_hbm, upn_ref, (up_sem.at[0], up_sem.at[1]), left)

    def fil_copy(r):
        return send(
            fil_hbm.at[:, quarter], all_ref.at[ctx, :, quarter], (fil_sem.at[0, r], fil_sem.at[1, r]),
            (group, lax.rem(ctx + r, n_ctx), fsdp, sub),
        )

    def cross_copy(r):
        held = lax.rem(ctx - r + n_ctx, n_ctx)
        return send(
            all_ref.at[held, :, quarter], all_ref.at[held, :, quarter],
            (cross_sem.at[0, r], cross_sem.at[1, r]), across_groups,
        )

    def swap_copy(r):
        held = lax.rem(ctx - r + n_ctx, n_ctx)
        return send(
            all_ref.at[held, :, kept], all_ref.at[held, :, kept],
            (swap_sem.at[0, r], swap_sem.at[1, r]), partner,
        )

    def z_copy(b):
        cols = columns(b)
        return send(
            z_ref.at[pl.ds(16, R - 16), cols], prev_ref.at[pl.ds(16, R - 16), cols],
            (z_sem.at[0, b], z_sem.at[1, b]), right,
        )

    def z_head_copy():
        return send(
            z_ref.at[pl.ds(0, 16), :], prev_ref.at[pl.ds(0, 16), :],
            (z_sem.at[0, blocks], z_sem.at[1, blocks]), right,
        )

    def q_copy(b):
        cols = columns(b)
        return send(
            feat_ref.at[0, :, cols], qn_ref.at[:, cols], (q_sem.at[0, b], q_sem.at[1, b]), left
        )

    def halo_copy(b):
        cols = columns(b)
        return send(
            halo_out.at[:, :, cols], halo_in.at[:, :, cols],
            (halo_sem.at[0, b], halo_sem.at[1, b]), left,
        )

    offsets = starts(lens_ref)
    age_down = age_of(offsets, base + down(R))
    gap = across(R) - down(R)
    lane = across(R)
    rim_gap = jnp.where(lane < 16 * KF, lane % 16 - 16 + lane // 16, 4 * R) - down(R)
    for j in range(KF):
        span = slice(j * R, (j + 1) * R)
        fwd_ref[:, span] = jnp.where((gap == -j) & (age_down >= j), 1.0, 0.0).astype(BF16)
    span = slice(KF * R, (KF + 1) * R)
    fwd_ref[:, span] = jnp.where((rim_gap == 0) & (age_down >= lane // 16), 1.0, 0.0).astype(BF16)
    stack_ref[:, KF * (R + 16) :, :] = jnp.zeros((3, R - 16 * KF, width), BF16)

    for load in loads[:2]:
        load.wait()

    tiles = packed([x_ref[i, R : R + 16, :].astype(F32)[8:16] for i in range(3)])
    for n in range(2):
        rim_out[n] = tiles[n]

    pl.semaphore_wait(barrier, count)

    @pl.when(has_right)
    def _():
        rim_copy().start()

    for r in range(1, n_ctx):
        fil_copy(r).start()

    @pl.when(has_left)
    def _():
        up_copy().start()

    @pl.when(jnp.logical_not(has_left))
    def _():
        rim_in[...] = jnp.zeros(rim_in.shape, BF16)
        prev_ref[...] = jnp.zeros(prev_ref.shape, BF16)

    @pl.when(jnp.logical_not(has_right))
    def _():
        upn_ref[...] = jnp.zeros(upn_ref.shape, BF16)
        qn_ref[...] = jnp.zeros(qn_ref.shape, BF16)
        halo_in[...] = jnp.zeros(halo_in.shape, BF16)


    def stack_near(i, source, near, cols):
        for j in range(KF):
            tile = wide(taps_ref[i, j : j + 1, cols])
            stack_ref[i, j * R : (j + 1) * R, :] = scaled(tile, source[i, near, cols])

    def stack_far(i, source, far, cols):
        for j in range(KF):
            tile = wide(taps_ref[i, j : j + 1, cols])
            at = KF * R + 16 * j
            stack_ref[i, at : at + 16, :] = scaled(tile, source[i, far, cols])

    def feat_block(b, carry):
        cols = columns(b)
        feats = [None] * 3
        for i in (1, 2, 0):
            stack_near(i, x_ref, slice(16, 16 + R), cols)
            total = dot(fwd_ref[:, : KF * R], stack_ref[i, : KF * R, :])
            head_ref[i, :, cols] = total[:16]
            feats[i] = total[16:].astype(BF16)
            feat_ref[i, 16:, cols] = feats[i]
        z_ref[16:, cols] = (feats[1].astype(F32) * feats[2].astype(F32)).astype(BF16)

        @pl.when(has_right)
        def _():
            z_copy(b).start()

        return carry

    lax.fori_loop(0, blocks, feat_block, 0)
    age_over = age_of(offsets, base + across(R))
    halo_age = age_of(offsets, base + R + lane % 16)
    halo_gap = jnp.where(lane < 16 * KF, lane % 16 + R - lane // 16, 4 * R) - down(R)
    for j in range(KF):
        span = slice(j * R, (j + 1) * R)
        bwd_ref[:, span] = jnp.where((gap == j) & (age_over >= j), 1.0, 0.0).astype(BF16)
        wide_gap = across(R + 16) - down(R) - 16
        shift_ref[span, :] = jnp.where((wide_gap == -j) & (age_down >= j), 1.0, 0.0).astype(BF16)
    sum_ref[...] = jnp.where(across(KF * R) // R == down(16), 1.0, 0.0).astype(BF16)
    span = slice(KF * R, (KF + 1) * R)
    bwd_ref[:, span] = jnp.where((halo_gap == 0) & (halo_age >= lane // 16), 1.0, 0.0).astype(BF16)
    for load in loads[2:]:
        load.wait()

    def kept_rows(table, mask):
        return jnp.where(mask, table.astype(F32), 0.0).astype(BF16)

    seg_down = segment_of(offsets, base + down(R))
    seg_over = segment_of(offsets, base + lane)
    seg_here, seg_next = segment_of(offsets, base + down(1)), segment_of(offsets, base + R + down(1))
    prev_mask = segment_of(offsets, base - R + lane) == seg_here
    next_mask = segment_of(offsets, base + R + lane) == seg_next
    prev_first[...] = kept_rows(first_ref[: 2 * LH], prev_mask)
    edge_second[...] = kept_rows(second_ref[: 2 * LH], seg_over == seg_here)
    next_second[...] = kept_rows(second_ref[: 2 * LH], next_mask)
    inv_w[:, : 2 * LH] = kept_rows(osecond_ref[:, : 2 * LH], seg_down == seg_here)
    inv_d[:, : 2 * LH] = kept_rows(ofirst_ref[:, : 2 * LH], seg_down == seg_next)
    for i, m in enumerate(LEVELS):
        at, to = 2 * LH + 128 * i, 128 * i
        mask = segment_of(offsets, base + lane // (2 * m) * (2 * m) + m) == seg_over
        own_first[to : to + 128] = kept_rows(first_ref[at : at + 128], mask)
        own_second[to : to + 128] = kept_rows(second_ref[at : at + 128], mask)
        mask = segment_of(offsets, base + down(R) // (2 * m) * (2 * m) + m) == seg_down
        inv_w[:, at : at + 128] = kept_rows(osecond_ref[:, at : at + 128], mask)
        inv_d[:, at : at + 128] = kept_rows(ofirst_ref[:, at : at + 128], mask)


    @pl.when(has_left)
    def _():
        rim_copy().wait_recv()

    def head_block(b, carry):
        cols = columns(b)
        for i, part in enumerate(unpacked([rim_in[n, :, cols] for n in range(2)])):
            x_ref[i, 0:16, cols] = jnp.concatenate([jnp.zeros(part.shape, F32), part], 0).astype(BF16)
        feats = [None] * 3
        for i in range(3):
            stack_far(i, x_ref, slice(0, 16), cols)
            feats[i] = (
                head_ref[i, :, cols] + dot(fwd_ref[0:16, KF * R :], stack_ref[i, KF * R :, :])
            ).astype(BF16)
            feat_ref[i, 0:16, cols] = feats[i]
        z_ref[0:16, cols] = (feats[1].astype(F32) * feats[2].astype(F32)).astype(BF16)

        @pl.when(has_left)
        def _():
            q_copy(b).start()

        return carry

    lax.fori_loop(0, blocks, head_block, 0)

    @pl.when(has_right)
    def _():
        z_head_copy().start()

    for r in range(1, n_ctx):
        fil_copy(r).wait_recv()
        cross_copy(r).start()

    def own_hat_block(b, carry):
        cols = columns(b)
        hz_ref[2 * LH :, cols] = dot(own_first[...], z_ref[:, cols]).astype(BF16)
        return carry

    lax.fori_loop(0, blocks, own_hat_block, 0)

    for r in range(1, n_ctx):
        cross_copy(r).wait_recv()
        swap_copy(r).start()
    for r in range(1, n_ctx):
        swap_copy(r).wait_recv()

    def fil_block(b, carry):
        cols = columns(b)
        taps = all_ref[:, :, cols].astype(F32).reshape(LH, width)
        fil_ref[0:8, cols] = taps[0:8]
        hf_ref[:, cols] = dot(ftaps_ref[...], taps.astype(BF16)).astype(BF16)
        return carry

    lax.fori_loop(0, blocks, fil_block, 0)

    proj_ref[...] = jnp.zeros(proj_ref.shape, F32)

    @pl.when(has_left)
    def _():
        z_head_copy().wait_recv()

    def mix_block(b, carry):
        cols = columns(b)

        @pl.when(has_left)
        def _():
            z_copy(b).wait_recv()

        hz_ref[: 2 * LH, cols] = dot(prev_first[...], prev_ref[:, cols]).astype(BF16)
        for (at, n), (f_re, f_im) in zip(level_rows(), tap_parts(hf_ref, cols)):
            z_re, z_im = hz_ref[at : at + n, cols], hz_ref[at + n : at + 2 * n, cols]
            prod_ref[at : at + n, :] = f_re * z_re - f_im * z_im
            prod_ref[at + n : at + 2 * n, :] = f_re * z_im + f_im * z_re
        w = dot(inv_w[...], prod_ref[...]) + fil_ref[0:1, cols] * z_ref[:, cols].astype(F32)
        w_ref[:, cols] = w
        weighted = feat_ref[0, :, cols].astype(F32) * w * dir_ref[:, cols]
        part = weighted[:, 0:128]
        for c in range(1, width // 128):
            part = part + weighted[:, c * 128 : (c + 1) * 128]
        proj_ref[...] += part
        return carry

    lax.fori_loop(0, blocks, mix_block, 0)

    for s in range(segs):
        part_ref[s : s + 1, :] = jnp.sum(
            jnp.where(seg_down == s, proj_ref[...], 0.0), axis=0, keepdims=True
        )

    def sum_copy(r):
        return send(part_ref, slots.at[r], (sum_send.at[r], sum_recv.at[r]), where(r))

    each_peer(lambda r: sum_copy(r).start())

    def shift_block(b, carry):
        cols = columns(b)
        for i in range(3):
            xs_ref[i, :, cols] = dot(shift_ref[...], x_ref[i, :, cols]).astype(BF16)
        return carry

    ids, id_row = jnp.zeros((segs, 1), jnp.int32), jnp.zeros((1, segs), jnp.int32)
    lengths = jnp.zeros((segs, 1), jnp.int32)
    for s in range(segs):
        ids = jnp.where(down(segs) == s, ids_ref[s], ids)
        id_row = jnp.where(across(segs) == s, ids_ref[s], id_row)
        lengths = jnp.where(down(segs) == s, lens_ref[s], lengths)
    lengths = lengths.astype(F32)
    same = down(segs) == across(segs)
    mates = jnp.where(ids == id_row, 1.0, 0.0)
    mate_count = jnp.sum(mates, axis=1, keepdims=True)
    hot = segment_of(offsets, base + down(2 * R)) == across(segs)
    lax.fori_loop(0, blocks, shift_block, 0)
    slots[0] = part_ref[...]
    each_peer(lambda r: sum_copy(r).wait_recv())

    def slot_of(d):
        back = (
            lax.rem(ctx - d // (n_fsdp * n_sub) + n_ctx, n_ctx) * n_fsdp
            + lax.rem(fsdp - d // n_sub % n_fsdp + n_fsdp, n_fsdp)
        )
        return slots[back * n_sub + lax.rem(sub - d % n_sub + n_sub, n_sub)]

    if count <= 32:
        found = [slot_of(d) for d in range(count)]
        while len(found) > 1:
            found = [a + b for a, b in zip(found[::2], found[1::2])]
        summed = found[0]
    else:
        summed = lax.fori_loop(
            0, count, lambda d, total: total + slot_of(d), jnp.zeros(part_ref.shape, F32)
        )
    scores = jnp.sum(summed, axis=1, keepdims=True) / lengths
    score_row = jnp.sum(jnp.where(same, scores, 0.0), axis=0, keepdims=True)
    means = jnp.sum(mates * score_row, axis=1, keepdims=True) / mate_count
    coef = (scores - means) / lengths
    coef_row = jnp.sum(jnp.where(same, coef, 0.0), axis=0, keepdims=True)
    coef_ref[...] = jnp.sum(jnp.where(hot, coef_row, 0.0), axis=1, keepdims=True)

    def own_block(b, carry):
        cols = columns(b)
        d_out = up_ref[:, cols].astype(F32) + coef_ref[0:R, :] * dir_ref[:, cols]
        da_ref[0, 0:R, cols] = (d_out * w_ref[:, cols]).astype(BF16)
        dw = (d_out * feat_ref[0, :, cols].astype(F32)).astype(BF16)
        dw_ref[:, cols] = dw
        edge = dot(edge_second[...], dw).astype(BF16)
        hd_ref[:, cols] = dot(own_second[...], dw).astype(BF16)
        for at, n in level_rows():
            if at == 0:
                d_re, d_im = edge[:n], edge[n:]
            else:
                to = at - 2 * LH
                d_re, d_im = hd_ref[to : to + n, cols], hd_ref[to + n : to + 2 * n, cols]
            z_re, z_im = hz_ref[at : at + n, cols], hz_ref[at + n : at + 2 * n, cols]
            prod_ref[at : at + n, :] = z_re * d_re + z_im * d_im
            prod_ref[at + n : at + 2 * n, :] = z_re * d_im - z_im * d_re
        whole = jnp.sum(dw.astype(F32) * z_ref[:, cols].astype(F32), axis=0, keepdims=True)
        dfil = dot(otaps_ref[...], prod_ref[...]) + jnp.where(down(LH) == 0, whole, 0.0)
        dfil_ref[:, :, cols] = dfil.reshape(n_ctx, shard, width).astype(BF16)
        return carry

    def grad_block(b, carry):
        cols = columns(b)

        @pl.when(has_right)
        def _():
            q_copy(b).wait_recv()

        d_next = upn_ref[:, cols].astype(F32) + coef_ref[R:, :] * dir_ref[:, cols]
        dw_next = (d_next * qn_ref[:, cols].astype(F32)).astype(BF16)
        after = dot(next_second[...], dw_next).astype(BF16)
        for (at, n), (f_re, f_im) in zip(level_rows(), tap_parts(hf_ref, cols)):
            if at == 0:
                d_re, d_im = after[:n], after[n:]
            else:
                to = at - 2 * LH
                d_re, d_im = hd_ref[to : to + n, cols], hd_ref[to + n : to + 2 * n, cols]
            prod_ref[at : at + n, :] = f_re * d_re + f_im * d_im
            prod_ref[at + n : at + 2 * n, :] = f_re * d_im - f_im * d_re
        dz = dot(inv_d[...], prod_ref[...]) + fil_ref[0:1, cols] * dw_ref[:, cols].astype(F32)
        da_ref[1, 0:R, cols] = (dz * feat_ref[2, :, cols].astype(F32)).astype(BF16)
        da_ref[2, 0:R, cols] = (dz * feat_ref[1, :, cols].astype(F32)).astype(BF16)

        tiles = packed([da_ref[i, 0:16, cols].astype(F32)[0:8] for i in range(3)])
        for n in range(2):
            halo_out[n, :, cols] = tiles[n]

        @pl.when(has_left)
        def _():
            halo_copy(b).start()

        return carry

    phases = n_ctx.bit_length() - 1

    def peer(p):
        other = ctx + (1 - 2 * lax.rem(ctx // 2**p, 2)) * 2**p
        return other, (group, other, fsdp, sub)

    def fil_swap():
        return send(dfil_ref.at[:, :, given], fil_a, (a_sem.at[0, 0], a_sem.at[1, 0]), partner)

    def fil_step(p, k):
        slot = n_ctx - (n_ctx >> p) + k
        other, device = peer(p)
        wanted = lax.rem(other, 2 ** (p + 1)) + k * 2 ** (p + 1)
        return send(fil_c.at[wanted], fil_b.at[slot], (b_sem.at[0, slot], b_sem.at[1, slot]), device)

    def fil_begin(p):
        for k in range(n_ctx >> (p + 1)):
            fil_step(p, k).start()

    def fil_end(p):
        totals = []
        for k in range(n_ctx >> (p + 1)):
            fil_step(p, k).wait()
            mine = lax.rem(ctx, 2 ** (p + 1)) + k * 2 ** (p + 1)
            slot = n_ctx - (n_ctx >> p) + k
            totals.append(fil_c[mine].astype(F32) + fil_b[slot].astype(F32))
            if p < phases - 1:
                fil_c[mine] = totals[-1].astype(BF16)
        return totals[0]

    tap_sets = ((tap0_ref, tap0_a, tap0_b, tap0_c), (tap1_ref, tap1_a, tap1_b, tap1_c))

    def tap_swap(c):
        own, got, _, _ = tap_sets[c]
        return send(own.at[:, :, given], got, (a_sem.at[0, 1 + c], a_sem.at[1, 1 + c]), partner)

    def tap_step(c, p):
        _, _, slots_of, running = tap_sets[c]
        return send(running, slots_of.at[p], (t_sem.at[0, c, p], t_sem.at[1, c, p]), peer(p)[1])

    def tap_first(c):
        tap_swap(c).wait()
        own, got, _, running = tap_sets[c]
        running[...] = (own[:, :, kept].astype(F32) + got[...].astype(F32)).astype(BF16)
        tap_step(c, 0).start()

    def tap_end(c, p):
        _, _, slots_of, running = tap_sets[c]
        tap_step(c, p).wait()
        total = running[...].astype(F32) + slots_of[p].astype(F32)
        if p < phases - 1:
            running[...] = total.astype(BF16)
        return total

    last = [
        send(fil_sum, out_ref.at[:, kept], (c_sem.at[0, 0], c_sem.at[1, 0]), partner),
        send(tap_sum, dtaps_ref.at[:, :, kept], (c_sem.at[0, 1], c_sem.at[1, 1]), partner),
    ]

    def tap_sums(i, b):
        cols = columns(b)
        own = da_ref[i, 0:R, cols]
        for j in range(KF):
            span = slice(j * R, (j + 1) * R)
            stack_ref[i, span, :] = own * xs_ref[i, span, cols]
        sums = dot(sum_ref[...], stack_ref[i, : KF * R, :])[0:8].astype(BF16)
        if i == 0:
            tap0_ref[0, :, cols] = sums
        else:
            tap1_ref[i - 1, :, cols] = sums

    def own_taps(b, carry):
        own_block(b, carry)
        tap_sums(0, b)
        return carry

    def grad_sums(b, carry):
        tap_sums(1, b)
        tap_sums(2, b)
        return carry

    def stream(i):
        def block(b, carry):
            cols = columns(b)
            stack_near(i, da_ref, slice(0, R), cols)
            stack_far(i, da_ref, slice(R, R + 16), cols)
            dx_ref[i, :, cols] = dot(bwd_ref[...], stack_ref[i]).astype(BF16)
            return carry

        lax.fori_loop(0, blocks, block, 0)

    def relay(c):
        first[c].wait()
        if c == 0:
            fil_c[...] = (dfil_ref[:, :, kept].astype(F32) + fil_a[...].astype(F32)).astype(BF16)
        else:
            i = c - 1
            tap_c[i] = (tap_ref[i, :, kept].astype(F32) + tap_a[i].astype(F32)).astype(BF16)
        for r in range(1, n_ctx):
            second(c, r).start()

    per_half = blocks // 2
    given_span = ((1 - sub) * per_half, (2 - sub) * per_half)
    kept_span = (sub * per_half, (1 + sub) * per_half)
    lax.fori_loop(*given_span, own_taps, 0)
    fil_swap().start()
    tap_swap(0).start()
    lax.fori_loop(*kept_span, own_taps, 0)
    fil_swap().wait()
    fil_c[...] = (dfil_ref[:, :, kept].astype(F32) + fil_a[...].astype(F32)).astype(BF16)
    fil_begin(0)
    tap_first(0)

    @pl.when(has_right)
    def _():
        up_copy().wait_recv()

    lax.fori_loop(*given_span, grad_block, 0)
    lax.fori_loop(*given_span, grad_sums, 0)
    tap_swap(1).start()
    lax.fori_loop(*kept_span, grad_block, 0)
    for p in range(phases - 1):
        fil_end(p)
        fil_begin(p + 1)
    lax.fori_loop(*kept_span, grad_sums, 0)
    tap_first(1)
    for p in range(phases - 1):
        tap_end(0, p)
        tap_step(0, p + 1).start()

    @pl.when(has_right)
    def _():
        for b in range(blocks):
            halo_copy(b).wait_recv()

    for i, part in enumerate(unpacked([halo_in[n] for n in range(2)])):
        da_ref[i, R:, :] = jnp.concatenate([part, jnp.zeros(part.shape, F32)], 0).astype(BF16)

    stream(0)
    for p in range(phases - 1):
        tap_end(1, p)
        tap_step(1, p + 1).start()
    stream(1)
    total = fil_end(phases - 1)
    fil_sum[...] = total
    out_ref[:, kept] = total
    last[0].start()
    stream(2)
    taps_total = tap_end(0, phases - 1)[:, :KF]
    tap_sum[0:1] = taps_total
    dtaps_ref[0:1, :, kept] = taps_total
    taps_total = tap_end(1, phases - 1)[:, :KF]
    tap_sum[1:3] = taps_total
    dtaps_ref[1:3, :, kept] = taps_total
    last[1].start()

    @pl.when(has_left)
    def _():
        up_copy().wait_send()
        for b in range(blocks):
            q_copy(b).wait_send()
            halo_copy(b).wait_send()

    @pl.when(has_right)
    def _():
        rim_copy().wait_send()
        z_head_copy().wait_send()
        for b in range(blocks):
            z_copy(b).wait_send()

    each_peer(lambda r: sum_copy(r).wait_send())
    for r in range(1, n_ctx):
        fil_copy(r).wait_send()
        cross_copy(r).wait_send()
        swap_copy(r).wait_send()
    last[0].wait()
    last[1].wait()


def store(dx_ref, dtaps_ref, dfil_ref, dx_out, dtaps_out, dfil_out, sems):
    copies = [
        pltpu.make_async_copy(dx_ref, dx_out, sems.at[0]),
        pltpu.make_async_copy(dtaps_ref, dtaps_out, sems.at[1]),
        pltpu.make_async_copy(dfil_ref, dfil_out, sems.at[2]),
    ]
    for copy in copies:
        copy.start()
    for copy in copies:
        copy.wait()


def local(sizes, streams, feat_taps, long_filter, upstream, score_dir, seg_lengths, list_ids):
    rows, chans = streams.shape[1:]
    assert rows == R
    width = min(1024, chans // 2)
    blocks = chans // width
    half = chans // 2
    n_ctx = sizes[0]
    count = sizes[0] * sizes[1] * sizes[2]
    shard = long_filter.shape[0]
    segs = seg_lengths.shape[0]
    vmem = pl.BlockSpec(memory_space=pltpu.VMEM)
    smem = pl.BlockSpec(memory_space=pltpu.SMEM)
    hbm = pl.BlockSpec(memory_space=pl.ANY)
    dma = pltpu.SemaphoreType.DMA
    own = ROWS - 2 * LH
    phases = n_ctx.bit_length() - 1
    assert n_ctx == 2**phases
    d_streams, d_taps, d_filter = pl.pallas_call(
        functools.partial(body, sizes, width),
        in_specs=[smem, smem, vmem] + [hbm] * 10,
        out_specs=[vmem] * 3,
        out_shape=[
            pltpu.VMEM((3, rows, chans), BF16),
            pltpu.VMEM((3, KF, chans), F32),
            pltpu.VMEM((shard, chans), F32),
        ],
        scratch_shapes=[
            pltpu.VMEM((3, R + 16, chans), BF16),
            pltpu.VMEM((3, KF, chans), F32),
            pltpu.VMEM((n_ctx, shard, chans), BF16),
            pltpu.VMEM((R, chans), BF16),
            pltpu.VMEM((R, chans), BF16),
            pltpu.VMEM((3, R, chans), BF16),
            pltpu.VMEM((R, chans), BF16),
            pltpu.VMEM((R, chans), BF16),
            pltpu.VMEM((R, chans), BF16),
            pltpu.VMEM((3, R + 16, chans), BF16),
            pltpu.VMEM((R, chans), BF16),
            pltpu.VMEM((R, chans), F32),
            *[pltpu.VMEM(t.shape, BF16) for t in TABLES],
            pltpu.VMEM((own, chans), BF16),
            pltpu.VMEM((3, KF * R, chans), BF16),
            pltpu.VMEM((16, KF * R), BF16),
            pltpu.VMEM((3, 16, chans), F32),
            *[pltpu.VMEM((2, 16, chans), BF16) for _ in range(4)],
            pltpu.VMEM((TAP_ROWS, chans), BF16),
            pltpu.VMEM((ROWS, chans), BF16),
            pltpu.VMEM((own, R), BF16),
            pltpu.VMEM((2 * LH, R), BF16),
            pltpu.VMEM((own, R), BF16),
            pltpu.VMEM((2 * LH, R), BF16),
            pltpu.VMEM((2 * LH, R), BF16),
            pltpu.VMEM((R, ROWS), BF16),
            pltpu.VMEM((R, ROWS), BF16),
            pltpu.VMEM((R, (KF + 1) * R), BF16),
            pltpu.VMEM((R, (KF + 1) * R), BF16),
            pltpu.VMEM((KF * R, R + 16), BF16),
            pltpu.VMEM((3, (KF + 1) * R, width), BF16),
            pltpu.VMEM((ROWS, width), BF16),
            pltpu.VMEM((R, 128), F32),
            pltpu.VMEM((2 * R, 1), F32),
            pltpu.VMEM((segs, 128), F32),
            pltpu.VMEM((count, segs, 128), F32),
            pltpu.VMEM((8, chans), F32),
            pltpu.VMEM((n_ctx, shard, chans), BF16),
            pltpu.VMEM((1, 8, chans), BF16),
            pltpu.VMEM((2, 8, chans), BF16),
            pltpu.VMEM((n_ctx, shard, half), BF16),
            pltpu.VMEM((n_ctx, shard, half), BF16),
            pltpu.VMEM((n_ctx, shard, half), BF16),
            pltpu.VMEM((shard, half), F32),
            pltpu.VMEM((1, 8, half), BF16),
            pltpu.VMEM((phases, 1, 8, half), BF16),
            pltpu.VMEM((1, 8, half), BF16),
            pltpu.VMEM((2, 8, half), BF16),
            pltpu.VMEM((phases, 2, 8, half), BF16),
            pltpu.VMEM((2, 8, half), BF16),
            pltpu.VMEM((3, KF, half), F32),
            dma((4 + len(TABLES),)),
            dma((2,)),
            dma((2, n_ctx)),
            dma((2, n_ctx)),
            dma((2, n_ctx)),
            dma((2,)),
            dma((2, blocks + 1)),
            dma((2, blocks)),
            dma((count,)),
            dma((count,)),
            dma((2, blocks)),
            dma((2, 3)),
            dma((2, n_ctx)),
            dma((2, 2, phases)),
            dma((2, 2)),
        ],
        compiler_params=pltpu.CompilerParams(
            collective_id=0, has_side_effects=True, vmem_limit_bytes=54 * 2**20
        ),
        name="hyena",
    )(
        seg_lengths, list_ids, score_dir[None, :], streams, feat_taps, long_filter, upstream,
        *[jnp.asarray(t, BF16) for t in TABLES],
    )
    return pl.pallas_call(
        store,
        in_specs=[hbm] * 3,
        out_specs=[hbm] * 3,
        out_shape=[
            jax.ShapeDtypeStruct((3, rows, chans), BF16),
            jax.ShapeDtypeStruct((3, KF, chans), F32),
            jax.ShapeDtypeStruct((shard, chans), F32),
        ],
        scratch_shapes=[dma((3,))],
        compiler_params=pltpu.CompilerParams(vmem_limit_bytes=2**20),
        name="store",
    )(d_streams, d_taps, d_filter)


def solution(mesh):
    placed = (
        P(None, ("groups", "ctx", "sub"), "fsdp"),
        P(None, None, "fsdp"),
        P("ctx", "fsdp"),
        P(("groups", "ctx", "sub"), "fsdp"),
        P("fsdp"),
        P("groups"),
        P("groups"),
    )
    sizes = (mesh.shape["ctx"], mesh.shape["fsdp"], mesh.shape["sub"])
    return jax.shard_map(
        functools.partial(local, sizes),
        mesh=mesh,
        in_specs=placed,
        out_specs=(
            P(None, ("groups", "ctx", "sub"), "fsdp"),
            P("groups", None, "fsdp"),
            P(("groups", "ctx"), "fsdp"),
        ),
        check_vma=False,
    )
```

```python
import functools

import jax
import jax.numpy as jnp
import numpy as np
from jax import lax
from jax.experimental import pallas as pl
from jax.experimental.pallas import tpu as pltpu
from jax.sharding import PartitionSpec as P

LH = 128
KF = 7
R = 128
F32 = jnp.float32
BF16 = jnp.bfloat16
MESH = pl.DeviceIdType.MESH

LEVELS = (64, 32, 16, 8, 4, 2, 1)
ROWS = 2 * LH + 128 * len(LEVELS)


def wave(m, positions):
    angle = np.pi * np.outer(2 * np.arange(m) + 1, positions) / (2 * m)
    return np.cos(angle), -np.sin(angle)


def tables():
    first, second, taps, out_first, out_second, out_taps = [], [], [], [], [], []
    for m in (LH,) + LEVELS:
        pairs = max(1, R // (2 * m))
        early, late, every = wave(m, np.arange(m)), wave(m, np.arange(m, 2 * m)), wave(m, np.arange(2 * m))
        span = min(2 * m, LH)
        for part in (0, 1):
            both = np.zeros((2, pairs * m, R))
            for g in range(pairs):
                rows = slice(g * m, (g + 1) * m)
                start = 2 * m * g
                both[0, rows, start : start + m] = early[part]
                both[1, rows, start + m if m < LH else 0 : start + 2 * m if m < LH else LH] = late[part]
            first.append(both[0])
            second.append(both[1])
            out_first.append(both[0].T / m)
            out_second.append(both[1].T / m)
            lag = np.zeros((m, LH))
            lag[:, 1:span] = every[part][:, 1:span]
            out_taps.append(np.tile(lag, (pairs, 1)).T / m)
            taps.append(np.tile(lag, (max(1, 16 // m), 1)))
    return (
        np.concatenate(first, 0), np.concatenate(second, 0), np.concatenate(taps, 0),
        np.concatenate(out_second, 1), np.concatenate(out_first, 1), np.concatenate(out_taps, 1),
    )


TABLES = [t.astype(np.float32) for t in tables()]
TAP_ROWS = TABLES[2].shape[0]


def starts(lens_ref):
    offsets, off = [], jnp.int32(0)
    for s in range(lens_ref.shape[0]):
        offsets.append(off)
        off = off + lens_ref[s]
    return offsets


def segment_of(offsets, position):
    seg = jnp.where(offsets[0] <= position, 0, -1)
    for off in offsets[1:]:
        seg = seg + jnp.where(off <= position, 1, 0)
    return seg


def age_of(offsets, position):
    start = jnp.zeros(position.shape, jnp.int32)
    for off in offsets:
        start = jnp.where(off <= position, off, start)
    return position - start


def down(rows):
    return lax.broadcasted_iota(jnp.int32, (rows, 1), 0)


def across(columns):
    return lax.broadcasted_iota(jnp.int32, (1, columns), 1)


def dot(a, b):
    return jnp.dot(a, b, preferred_element_type=F32)


def send(src, dst, sems, device):
    return pltpu.make_async_remote_copy(
        src_ref=src, dst_ref=dst, send_sem=sems[0], recv_sem=sems[1], device_id=device,
        device_id_type=MESH,
    )


def wide(row):
    return jnp.broadcast_to(row, (16, row.shape[1])).astype(BF16)


def scaled(tile, block):
    rows, width = block.shape
    return (block.reshape(rows // 16, 16, width) * tile[None]).reshape(rows, width)


def packed(parts):
    wide_parts = [part.astype(F32) for part in parts] + [jnp.zeros(parts[0].shape, F32)]
    return [jnp.concatenate(wide_parts[n : n + 2], 0).astype(BF16) for n in (0, 2)]


def unpacked(tiles):
    both, one = tiles[0].astype(F32), tiles[1].astype(F32)
    return [both[0:8], both[8:16], one[0:8]]


def tap_parts(hat_ref, cols):
    parts, at = [], 0
    for m in (LH,) + LEVELS:
        rows, want = max(m, 16), max(64, m)
        pair = []
        for _ in range(2):
            piece = hat_ref[at : at + rows, cols]
            pair.append(piece if rows == want else jnp.concatenate([piece] * (want // rows), 0))
            at += rows
        parts.append(pair)
    return parts


def level_rows():
    spans, at = [], 0
    for m in (LH,) + LEVELS:
        half = max(64, m)
        spans.append((at, half))
        at += 2 * half
    return spans


def body(
    sizes, width,
    lens_ref, ids_ref, dir_ref, x_hbm, taps_hbm, fil_hbm, up_hbm, *refs,
):
    constants, refs = refs[:6], refs[6:]
    (
    dx_ref, dtaps_ref, out_ref,
    x_ref, taps_ref, all_ref, up_ref, upn_ref, feat_ref, z_ref, prev_ref, qn_ref, da_ref, dw_ref, w_ref,
    first_ref, second_ref, ftaps_ref, osecond_ref, ofirst_ref, otaps_ref, hd_ref, xs_ref, sum_ref, head_ref, rim_out, rim_in, halo_out, halo_in,
    hf_ref, hz_ref, own_first, prev_first, own_second, edge_second, next_second, inv_w, inv_d,
    fwd_ref, bwd_ref, shift_ref, stack_ref, prod_ref, proj_ref, coef_ref,
    part_ref, slots, fil_ref, dfil_ref, tap0_ref, tap1_ref, fil_a, fil_b, fil_c, fil_sum, tap0_a, tap0_b, tap0_c,
    tap1_a, tap1_b, tap1_c, tap_sum,
    load_sem, rim_sem, fil_sem, cross_sem, swap_sem, up_sem, z_sem, q_sem, sum_send, sum_recv, halo_sem,
    a_sem, b_sem, t_sem, c_sem,
    ) = refs
    n_ctx, n_fsdp, n_sub = sizes
    group, ctx = lax.axis_index("groups"), lax.axis_index("ctx")
    fsdp, sub = lax.axis_index("fsdp"), lax.axis_index("sub")
    chans = dir_ref.shape[1]
    half = chans // 2
    blocks = chans // width
    shard = fil_hbm.shape[0]
    segs = lens_ref.shape[0]
    line = ctx * 2 + sub
    base = line * R
    left = (group, (line - 1) // 2, fsdp, 1 - sub)
    right = (group, (line + 1) // 2, fsdp, 1 - sub)
    partner = (group, ctx, fsdp, 1 - sub)
    across_groups = (1 - group, ctx, fsdp, sub)
    has_left, has_right = line > 0, line < 2 * n_ctx - 1
    count = n_ctx * n_fsdp * n_sub

    def where(r):
        return (
            group,
            lax.rem(ctx + r // (n_fsdp * n_sub), n_ctx),
            lax.rem(fsdp + r // n_sub % n_fsdp, n_fsdp),
            lax.rem(sub + r % n_sub, n_sub),
        )

    def each_peer(step):
        if count <= 32:
            for r in range(1, count):
                step(r)
        else:
            lax.fori_loop(1, count, lambda r, carry: (step(r), carry)[1], 0)

    kept = pl.ds(pl.multiple_of(sub * half, half), half)
    quarter = pl.ds(pl.multiple_of((sub * 2 + group) * (half // 2), half // 2), half // 2)
    given = pl.ds(pl.multiple_of((1 - sub) * half, half), half)

    def columns(b):
        return pl.ds(pl.multiple_of(b * width, width), width)

    barrier = pltpu.get_barrier_semaphore()

    def greet(r):
        pl.semaphore_signal(barrier, inc=1, device_id=where(r), device_id_type=MESH)

    pl.semaphore_signal(barrier, inc=1, device_id=across_groups, device_id_type=MESH)
    each_peer(greet)
    held = (first_ref, second_ref, ftaps_ref, osecond_ref, ofirst_ref, otaps_ref)
    loads = [
        pltpu.make_async_copy(x_hbm, x_ref.at[:, pl.ds(16, R), :], load_sem.at[0]),
        pltpu.make_async_copy(taps_hbm, taps_ref, load_sem.at[1]),
        pltpu.make_async_copy(fil_hbm, all_ref.at[ctx], load_sem.at[2]),
        pltpu.make_async_copy(up_hbm, up_ref, load_sem.at[3]),
    ] + [
        pltpu.make_async_copy(source, target, load_sem.at[4 + n])
        for n, (source, target) in enumerate(zip(constants, held))
    ]
    for load in loads:
        load.start()

    def rim_copy():
        return send(
            rim_out, rim_in, (rim_sem.at[0], rim_sem.at[1]), right,
        )

    def up_copy():
        return send(up_hbm, upn_ref, (up_sem.at[0], up_sem.at[1]), left)

    def fil_copy(r):
        return send(
            fil_hbm.at[:, quarter], all_ref.at[ctx, :, quarter], (fil_sem.at[0, r], fil_sem.at[1, r]),
            (group, lax.rem(ctx + r, n_ctx), fsdp, sub),
        )

    def cross_copy(r):
        held = lax.rem(ctx - r + n_ctx, n_ctx)
        return send(
            all_ref.at[held, :, quarter], all_ref.at[held, :, quarter],
            (cross_sem.at[0, r], cross_sem.at[1, r]), across_groups,
        )

    def swap_copy(r):
        held = lax.rem(ctx - r + n_ctx, n_ctx)
        return send(
            all_ref.at[held, :, kept], all_ref.at[held, :, kept],
            (swap_sem.at[0, r], swap_sem.at[1, r]), partner,
        )

    def z_copy(b):
        cols = columns(b)
        return send(
            z_ref.at[pl.ds(16, R - 16), cols], prev_ref.at[pl.ds(16, R - 16), cols],
            (z_sem.at[0, b], z_sem.at[1, b]), right,
        )

    def z_head_copy():
        return send(
            z_ref.at[pl.ds(0, 16), :], prev_ref.at[pl.ds(0, 16), :],
            (z_sem.at[0, blocks], z_sem.at[1, blocks]), right,
        )

    def q_copy(b):
        cols = columns(b)
        return send(
            feat_ref.at[0, :, cols], qn_ref.at[:, cols], (q_sem.at[0, b], q_sem.at[1, b]), left
        )

    def halo_copy(b):
        cols = columns(b)
        return send(
            halo_out.at[:, :, cols], halo_in.at[:, :, cols],
            (halo_sem.at[0, b], halo_sem.at[1, b]), left,
        )

    offsets = starts(lens_ref)
    age_down = age_of(offsets, base + down(R))
    gap = across(R) - down(R)
    lane = across(R)
    rim_gap = jnp.where(lane < 16 * KF, lane % 16 - 16 + lane // 16, 4 * R) - down(R)
    for j in range(KF):
        span = slice(j * R, (j + 1) * R)
        fwd_ref[:, span] = jnp.where((gap == -j) & (age_down >= j), 1.0, 0.0).astype(BF16)
    span = slice(KF * R, (KF + 1) * R)
    fwd_ref[:, span] = jnp.where((rim_gap == 0) & (age_down >= lane // 16), 1.0, 0.0).astype(BF16)
    stack_ref[:, KF * (R + 16) :, :] = jnp.zeros((3, R - 16 * KF, width), BF16)

    for load in loads[:2]:
        load.wait()

    tiles = packed([x_ref[i, R : R + 16, :].astype(F32)[8:16] for i in range(3)])
    for n in range(2):
        rim_out[n] = tiles[n]

    pl.semaphore_wait(barrier, count)

    @pl.when(has_right)
    def _():
        rim_copy().start()

    for r in range(1, n_ctx):
        fil_copy(r).start()

    @pl.when(has_left)
    def _():
        up_copy().start()

    @pl.when(jnp.logical_not(has_left))
    def _():
        rim_in[...] = jnp.zeros(rim_in.shape, BF16)
        prev_ref[...] = jnp.zeros(prev_ref.shape, BF16)

    @pl.when(jnp.logical_not(has_right))
    def _():
        upn_ref[...] = jnp.zeros(upn_ref.shape, BF16)
        qn_ref[...] = jnp.zeros(qn_ref.shape, BF16)
        halo_in[...] = jnp.zeros(halo_in.shape, BF16)


    def stack_near(i, source, near, cols):
        for j in range(KF):
            tile = wide(taps_ref[i, j : j + 1, cols])
            stack_ref[i, j * R : (j + 1) * R, :] = scaled(tile, source[i, near, cols])

    def stack_far(i, source, far, cols):
        for j in range(KF):
            tile = wide(taps_ref[i, j : j + 1, cols])
            at = KF * R + 16 * j
            stack_ref[i, at : at + 16, :] = scaled(tile, source[i, far, cols])

    def feat_block(b, carry):
        cols = columns(b)
        feats = [None] * 3
        for i in (1, 2, 0):
            stack_near(i, x_ref, slice(16, 16 + R), cols)
            total = dot(fwd_ref[:, : KF * R], stack_ref[i, : KF * R, :])
            head_ref[i, :, cols] = total[:16]
            feats[i] = total[16:].astype(BF16)
            feat_ref[i, 16:, cols] = feats[i]
        z_ref[16:, cols] = (feats[1].astype(F32) * feats[2].astype(F32)).astype(BF16)

        @pl.when(has_right)
        def _():
            z_copy(b).start()

        return carry

    lax.fori_loop(0, blocks, feat_block, 0)
    age_over = age_of(offsets, base + across(R))
    halo_age = age_of(offsets, base + R + lane % 16)
    halo_gap = jnp.where(lane < 16 * KF, lane % 16 + R - lane // 16, 4 * R) - down(R)
    for j in range(KF):
        span = slice(j * R, (j + 1) * R)
        bwd_ref[:, span] = jnp.where((gap == j) & (age_over >= j), 1.0, 0.0).astype(BF16)
        wide_gap = across(R + 16) - down(R) - 16
        shift_ref[span, :] = jnp.where((wide_gap == -j) & (age_down >= j), 1.0, 0.0).astype(BF16)
    sum_ref[...] = jnp.where(across(KF * R) // R == down(16), 1.0, 0.0).astype(BF16)
    span = slice(KF * R, (KF + 1) * R)
    bwd_ref[:, span] = jnp.where((halo_gap == 0) & (halo_age >= lane // 16), 1.0, 0.0).astype(BF16)
    for load in loads[2:]:
        load.wait()

    def kept_rows(table, mask):
        return jnp.where(mask, table.astype(F32), 0.0).astype(BF16)

    seg_down = segment_of(offsets, base + down(R))
    seg_over = segment_of(offsets, base + lane)
    seg_here, seg_next = segment_of(offsets, base + down(1)), segment_of(offsets, base + R + down(1))
    prev_mask = segment_of(offsets, base - R + lane) == seg_here
    next_mask = segment_of(offsets, base + R + lane) == seg_next
    prev_first[...] = kept_rows(first_ref[: 2 * LH], prev_mask)
    edge_second[...] = kept_rows(second_ref[: 2 * LH], seg_over == seg_here)
    next_second[...] = kept_rows(second_ref[: 2 * LH], next_mask)
    inv_w[:, : 2 * LH] = kept_rows(osecond_ref[:, : 2 * LH], seg_down == seg_here)
    inv_d[:, : 2 * LH] = kept_rows(ofirst_ref[:, : 2 * LH], seg_down == seg_next)
    for i, m in enumerate(LEVELS):
        at, to = 2 * LH + 128 * i, 128 * i
        mask = segment_of(offsets, base + lane // (2 * m) * (2 * m) + m) == seg_over
        own_first[to : to + 128] = kept_rows(first_ref[at : at + 128], mask)
        own_second[to : to + 128] = kept_rows(second_ref[at : at + 128], mask)
        mask = segment_of(offsets, base + down(R) // (2 * m) * (2 * m) + m) == seg_down
        inv_w[:, at : at + 128] = kept_rows(osecond_ref[:, at : at + 128], mask)
        inv_d[:, at : at + 128] = kept_rows(ofirst_ref[:, at : at + 128], mask)


    @pl.when(has_left)
    def _():
        rim_copy().wait_recv()

    def head_block(b, carry):
        cols = columns(b)
        for i, part in enumerate(unpacked([rim_in[n, :, cols] for n in range(2)])):
            x_ref[i, 0:16, cols] = jnp.concatenate([jnp.zeros(part.shape, F32), part], 0).astype(BF16)
        feats = [None] * 3
        for i in range(3):
            stack_far(i, x_ref, slice(0, 16), cols)
            feats[i] = (
                head_ref[i, :, cols] + dot(fwd_ref[0:16, KF * R :], stack_ref[i, KF * R :, :])
            ).astype(BF16)
            feat_ref[i, 0:16, cols] = feats[i]
        z_ref[0:16, cols] = (feats[1].astype(F32) * feats[2].astype(F32)).astype(BF16)

        @pl.when(has_left)
        def _():
            q_copy(b).start()

        return carry

    lax.fori_loop(0, blocks, head_block, 0)

    @pl.when(has_right)
    def _():
        z_head_copy().start()

    for r in range(1, n_ctx):
        fil_copy(r).wait_recv()
        cross_copy(r).start()

    def own_hat_block(b, carry):
        cols = columns(b)
        hz_ref[2 * LH :, cols] = dot(own_first[...], z_ref[:, cols]).astype(BF16)
        return carry

    lax.fori_loop(0, blocks, own_hat_block, 0)

    for r in range(1, n_ctx):
        cross_copy(r).wait_recv()
        swap_copy(r).start()
    for r in range(1, n_ctx):
        swap_copy(r).wait_recv()

    def fil_block(b, carry):
        cols = columns(b)
        taps = all_ref[:, :, cols].astype(F32).reshape(LH, width)
        fil_ref[0:8, cols] = taps[0:8]
        hf_ref[:, cols] = dot(ftaps_ref[...], taps.astype(BF16)).astype(BF16)
        return carry

    lax.fori_loop(0, blocks, fil_block, 0)

    proj_ref[...] = jnp.zeros(proj_ref.shape, F32)

    @pl.when(has_left)
    def _():
        z_head_copy().wait_recv()

    def mix_block(b, carry):
        cols = columns(b)

        @pl.when(has_left)
        def _():
            z_copy(b).wait_recv()

        hz_ref[: 2 * LH, cols] = dot(prev_first[...], prev_ref[:, cols]).astype(BF16)
        for (at, n), (f_re, f_im) in zip(level_rows(), tap_parts(hf_ref, cols)):
            z_re, z_im = hz_ref[at : at + n, cols], hz_ref[at + n : at + 2 * n, cols]
            prod_ref[at : at + n, :] = f_re * z_re - f_im * z_im
            prod_ref[at + n : at + 2 * n, :] = f_re * z_im + f_im * z_re
        w = dot(inv_w[...], prod_ref[...]) + fil_ref[0:1, cols] * z_ref[:, cols].astype(F32)
        w_ref[:, cols] = w
        weighted = feat_ref[0, :, cols].astype(F32) * w * dir_ref[:, cols]
        part = weighted[:, 0:128]
        for c in range(1, width // 128):
            part = part + weighted[:, c * 128 : (c + 1) * 128]
        proj_ref[...] += part
        return carry

    lax.fori_loop(0, blocks, mix_block, 0)

    for s in range(segs):
        part_ref[s : s + 1, :] = jnp.sum(
            jnp.where(seg_down == s, proj_ref[...], 0.0), axis=0, keepdims=True
        )

    def sum_copy(r):
        return send(part_ref, slots.at[r], (sum_send.at[r], sum_recv.at[r]), where(r))

    each_peer(lambda r: sum_copy(r).start())

    def shift_block(b, carry):
        cols = columns(b)
        for i in range(3):
            xs_ref[i, :, cols] = dot(shift_ref[...], x_ref[i, :, cols]).astype(BF16)
        return carry

    ids, id_row = jnp.zeros((segs, 1), jnp.int32), jnp.zeros((1, segs), jnp.int32)
    lengths = jnp.zeros((segs, 1), jnp.int32)
    for s in range(segs):
        ids = jnp.where(down(segs) == s, ids_ref[s], ids)
        id_row = jnp.where(across(segs) == s, ids_ref[s], id_row)
        lengths = jnp.where(down(segs) == s, lens_ref[s], lengths)
    lengths = lengths.astype(F32)
    same = down(segs) == across(segs)
    mates = jnp.where(ids == id_row, 1.0, 0.0)
    mate_count = jnp.sum(mates, axis=1, keepdims=True)
    hot = segment_of(offsets, base + down(2 * R)) == across(segs)
    lax.fori_loop(0, blocks, shift_block, 0)
    slots[0] = part_ref[...]
    each_peer(lambda r: sum_copy(r).wait_recv())

    def slot_of(d):
        back = (
            lax.rem(ctx - d // (n_fsdp * n_sub) + n_ctx, n_ctx) * n_fsdp
            + lax.rem(fsdp - d // n_sub % n_fsdp + n_fsdp, n_fsdp)
        )
        return slots[back * n_sub + lax.rem(sub - d % n_sub + n_sub, n_sub)]

    if count <= 32:
        found = [slot_of(d) for d in range(count)]
        while len(found) > 1:
            found = [a + b for a, b in zip(found[::2], found[1::2])]
        summed = found[0]
    else:
        summed = lax.fori_loop(
            0, count, lambda d, total: total + slot_of(d), jnp.zeros(part_ref.shape, F32)
        )
    scores = jnp.sum(summed, axis=1, keepdims=True) / lengths
    score_row = jnp.sum(jnp.where(same, scores, 0.0), axis=0, keepdims=True)
    means = jnp.sum(mates * score_row, axis=1, keepdims=True) / mate_count
    coef = (scores - means) / lengths
    coef_row = jnp.sum(jnp.where(same, coef, 0.0), axis=0, keepdims=True)
    coef_ref[...] = jnp.sum(jnp.where(hot, coef_row, 0.0), axis=1, keepdims=True)

    def own_block(b, carry):
        cols = columns(b)
        d_out = up_ref[:, cols].astype(F32) + coef_ref[0:R, :] * dir_ref[:, cols]
        da_ref[0, 0:R, cols] = (d_out * w_ref[:, cols]).astype(BF16)
        dw = (d_out * feat_ref[0, :, cols].astype(F32)).astype(BF16)
        dw_ref[:, cols] = dw
        edge = dot(edge_second[...], dw).astype(BF16)
        hd_ref[:, cols] = dot(own_second[...], dw).astype(BF16)
        for at, n in level_rows():
            if at == 0:
                d_re, d_im = edge[:n], edge[n:]
            else:
                to = at - 2 * LH
                d_re, d_im = hd_ref[to : to + n, cols], hd_ref[to + n : to + 2 * n, cols]
            z_re, z_im = hz_ref[at : at + n, cols], hz_ref[at + n : at + 2 * n, cols]
            prod_ref[at : at + n, :] = z_re * d_re + z_im * d_im
            prod_ref[at + n : at + 2 * n, :] = z_re * d_im - z_im * d_re
        whole = jnp.sum(dw.astype(F32) * z_ref[:, cols].astype(F32), axis=0, keepdims=True)
        dfil = dot(otaps_ref[...], prod_ref[...]) + jnp.where(down(LH) == 0, whole, 0.0)
        dfil_ref[:, :, cols] = dfil.reshape(n_ctx, shard, width).astype(BF16)
        return carry

    def grad_block(b, carry):
        cols = columns(b)

        @pl.when(has_right)
        def _():
            q_copy(b).wait_recv()

        d_next = upn_ref[:, cols].astype(F32) + coef_ref[R:, :] * dir_ref[:, cols]
        dw_next = (d_next * qn_ref[:, cols].astype(F32)).astype(BF16)
        after = dot(next_second[...], dw_next).astype(BF16)
        for (at, n), (f_re, f_im) in zip(level_rows(), tap_parts(hf_ref, cols)):
            if at == 0:
                d_re, d_im = after[:n], after[n:]
            else:
                to = at - 2 * LH
                d_re, d_im = hd_ref[to : to + n, cols], hd_ref[to + n : to + 2 * n, cols]
            prod_ref[at : at + n, :] = f_re * d_re + f_im * d_im
            prod_ref[at + n : at + 2 * n, :] = f_re * d_im - f_im * d_re
        dz = dot(inv_d[...], prod_ref[...]) + fil_ref[0:1, cols] * dw_ref[:, cols].astype(F32)
        da_ref[1, 0:R, cols] = (dz * feat_ref[2, :, cols].astype(F32)).astype(BF16)
        da_ref[2, 0:R, cols] = (dz * feat_ref[1, :, cols].astype(F32)).astype(BF16)

        tiles = packed([da_ref[i, 0:16, cols].astype(F32)[0:8] for i in range(3)])
        for n in range(2):
            halo_out[n, :, cols] = tiles[n]

        @pl.when(has_left)
        def _():
            halo_copy(b).start()

        return carry

    phases = n_ctx.bit_length() - 1

    def peer(p):
        other = ctx + (1 - 2 * lax.rem(ctx // 2**p, 2)) * 2**p
        return other, (group, other, fsdp, sub)

    def fil_swap():
        return send(dfil_ref.at[:, :, given], fil_a, (a_sem.at[0, 0], a_sem.at[1, 0]), partner)

    def fil_step(p, k):
        slot = n_ctx - (n_ctx >> p) + k
        other, device = peer(p)
        wanted = lax.rem(other, 2 ** (p + 1)) + k * 2 ** (p + 1)
        return send(fil_c.at[wanted], fil_b.at[slot], (b_sem.at[0, slot], b_sem.at[1, slot]), device)

    def fil_begin(p):
        for k in range(n_ctx >> (p + 1)):
            fil_step(p, k).start()

    def fil_end(p):
        totals = []
        for k in range(n_ctx >> (p + 1)):
            fil_step(p, k).wait()
            mine = lax.rem(ctx, 2 ** (p + 1)) + k * 2 ** (p + 1)
            slot = n_ctx - (n_ctx >> p) + k
            totals.append(fil_c[mine].astype(F32) + fil_b[slot].astype(F32))
            if p < phases - 1:
                fil_c[mine] = totals[-1].astype(BF16)
        return totals[0]

    tap_sets = ((tap0_ref, tap0_a, tap0_b, tap0_c), (tap1_ref, tap1_a, tap1_b, tap1_c))

    def tap_swap(c):
        own, got, _, _ = tap_sets[c]
        return send(own.at[:, :, given], got, (a_sem.at[0, 1 + c], a_sem.at[1, 1 + c]), partner)

    def tap_step(c, p):
        _, _, slots_of, running = tap_sets[c]
        return send(running, slots_of.at[p], (t_sem.at[0, c, p], t_sem.at[1, c, p]), peer(p)[1])

    def tap_first(c):
        tap_swap(c).wait()
        own, got, _, running = tap_sets[c]
        running[...] = (own[:, :, kept].astype(F32) + got[...].astype(F32)).astype(BF16)
        tap_step(c, 0).start()

    def tap_end(c, p):
        _, _, slots_of, running = tap_sets[c]
        tap_step(c, p).wait()
        total = running[...].astype(F32) + slots_of[p].astype(F32)
        if p < phases - 1:
            running[...] = total.astype(BF16)
        return total

    last = [
        send(fil_sum, out_ref.at[:, kept], (c_sem.at[0, 0], c_sem.at[1, 0]), partner),
        send(tap_sum, dtaps_ref.at[:, :, kept], (c_sem.at[0, 1], c_sem.at[1, 1]), partner),
    ]

    def tap_sums(i, b):
        cols = columns(b)
        own = da_ref[i, 0:R, cols]
        for j in range(KF):
            span = slice(j * R, (j + 1) * R)
            stack_ref[i, span, :] = own * xs_ref[i, span, cols]
        sums = dot(sum_ref[...], stack_ref[i, : KF * R, :])[0:8].astype(BF16)
        if i == 0:
            tap0_ref[0, :, cols] = sums
        else:
            tap1_ref[i - 1, :, cols] = sums

    def own_taps(b, carry):
        own_block(b, carry)
        tap_sums(0, b)
        return carry

    def grad_sums(b, carry):
        tap_sums(1, b)
        tap_sums(2, b)
        return carry

    def stream_block(i, b):
        cols = columns(b)
        stack_near(i, da_ref, slice(0, R), cols)
        stack_far(i, da_ref, slice(R, R + 16), cols)
        dx_ref[i, :, cols] = dot(bwd_ref[...], stack_ref[i]).astype(BF16)

    def first_stream(b, carry):
        cols = columns(b)

        @pl.when(has_right)
        def _():
            halo_copy(b).wait_recv()

        for i, part in enumerate(unpacked([halo_in[n, :, cols] for n in range(2)])):
            da_ref[i, R:, cols] = jnp.concatenate([part, jnp.zeros(part.shape, F32)], 0).astype(BF16)
        stream_block(0, b)
        return carry

    def stream(i):
        lax.fori_loop(0, blocks, lambda b, carry: (stream_block(i, b), carry)[1], 0)

    per_half = blocks // 2
    given_span = ((1 - sub) * per_half, (2 - sub) * per_half)
    kept_span = (sub * per_half, (1 + sub) * per_half)
    lax.fori_loop(*given_span, own_taps, 0)
    fil_swap().start()
    tap_swap(0).start()
    lax.fori_loop(*kept_span, own_taps, 0)
    fil_swap().wait()
    fil_c[...] = (dfil_ref[:, :, kept].astype(F32) + fil_a[...].astype(F32)).astype(BF16)
    fil_begin(0)
    tap_first(0)

    @pl.when(has_right)
    def _():
        up_copy().wait_recv()

    lax.fori_loop(*given_span, grad_block, 0)
    lax.fori_loop(*given_span, grad_sums, 0)
    tap_swap(1).start()
    lax.fori_loop(*kept_span, grad_block, 0)
    for p in range(phases - 1):
        fil_end(p)
        fil_begin(p + 1)
    lax.fori_loop(*kept_span, grad_sums, 0)
    tap_first(1)
    for p in range(phases - 1):
        tap_end(0, p)
        tap_step(0, p + 1).start()

    lax.fori_loop(*kept_span, first_stream, 0)
    lax.fori_loop(*given_span, first_stream, 0)
    for p in range(phases - 1):
        tap_end(1, p)
        tap_step(1, p + 1).start()
    stream(1)
    total = fil_end(phases - 1)
    fil_sum[...] = total
    out_ref[:, kept] = total
    last[0].start()
    stream(2)
    taps_total = tap_end(0, phases - 1)[:, :KF]
    tap_sum[0:1] = taps_total
    dtaps_ref[0:1, :, kept] = taps_total
    taps_total = tap_end(1, phases - 1)[:, :KF]
    tap_sum[1:3] = taps_total
    dtaps_ref[1:3, :, kept] = taps_total
    last[1].start()

    @pl.when(has_left)
    def _():
        up_copy().wait_send()
        for b in range(blocks):
            q_copy(b).wait_send()
            halo_copy(b).wait_send()

    @pl.when(has_right)
    def _():
        rim_copy().wait_send()
        z_head_copy().wait_send()
        for b in range(blocks):
            z_copy(b).wait_send()

    each_peer(lambda r: sum_copy(r).wait_send())
    for r in range(1, n_ctx):
        fil_copy(r).wait_send()
        cross_copy(r).wait_send()
        swap_copy(r).wait_send()
    last[0].wait()
    last[1].wait()


def store(dx_ref, dtaps_ref, dfil_ref, dx_out, dtaps_out, dfil_out, sems):
    copies = [
        pltpu.make_async_copy(dx_ref, dx_out, sems.at[0]),
        pltpu.make_async_copy(dtaps_ref, dtaps_out, sems.at[1]),
        pltpu.make_async_copy(dfil_ref, dfil_out, sems.at[2]),
    ]
    for copy in copies:
        copy.start()
    for copy in copies:
        copy.wait()


def local(sizes, streams, feat_taps, long_filter, upstream, score_dir, seg_lengths, list_ids):
    rows, chans = streams.shape[1:]
    assert rows == R
    width = min(1024, chans // 2)
    blocks = chans // width
    half = chans // 2
    n_ctx = sizes[0]
    count = sizes[0] * sizes[1] * sizes[2]
    shard = long_filter.shape[0]
    segs = seg_lengths.shape[0]
    vmem = pl.BlockSpec(memory_space=pltpu.VMEM)
    smem = pl.BlockSpec(memory_space=pltpu.SMEM)
    hbm = pl.BlockSpec(memory_space=pl.ANY)
    dma = pltpu.SemaphoreType.DMA
    own = ROWS - 2 * LH
    phases = n_ctx.bit_length() - 1
    assert n_ctx == 2**phases
    d_streams, d_taps, d_filter = pl.pallas_call(
        functools.partial(body, sizes, width),
        in_specs=[smem, smem, vmem] + [hbm] * 10,
        out_specs=[vmem] * 3,
        out_shape=[
            pltpu.VMEM((3, rows, chans), BF16),
            pltpu.VMEM((3, KF, chans), F32),
            pltpu.VMEM((shard, chans), F32),
        ],
        scratch_shapes=[
            pltpu.VMEM((3, R + 16, chans), BF16),
            pltpu.VMEM((3, KF, chans), F32),
            pltpu.VMEM((n_ctx, shard, chans), BF16),
            pltpu.VMEM((R, chans), BF16),
            pltpu.VMEM((R, chans), BF16),
            pltpu.VMEM((3, R, chans), BF16),
            pltpu.VMEM((R, chans), BF16),
            pltpu.VMEM((R, chans), BF16),
            pltpu.VMEM((R, chans), BF16),
            pltpu.VMEM((3, R + 16, chans), BF16),
            pltpu.VMEM((R, chans), BF16),
            pltpu.VMEM((R, chans), F32),
            *[pltpu.VMEM(t.shape, BF16) for t in TABLES],
            pltpu.VMEM((own, chans), BF16),
            pltpu.VMEM((3, KF * R, chans), BF16),
            pltpu.VMEM((16, KF * R), BF16),
            pltpu.VMEM((3, 16, chans), F32),
            *[pltpu.VMEM((2, 16, chans), BF16) for _ in range(4)],
            pltpu.VMEM((TAP_ROWS, chans), BF16),
            pltpu.VMEM((ROWS, chans), BF16),
            pltpu.VMEM((own, R), BF16),
            pltpu.VMEM((2 * LH, R), BF16),
            pltpu.VMEM((own, R), BF16),
            pltpu.VMEM((2 * LH, R), BF16),
            pltpu.VMEM((2 * LH, R), BF16),
            pltpu.VMEM((R, ROWS), BF16),
            pltpu.VMEM((R, ROWS), BF16),
            pltpu.VMEM((R, (KF + 1) * R), BF16),
            pltpu.VMEM((R, (KF + 1) * R), BF16),
            pltpu.VMEM((KF * R, R + 16), BF16),
            pltpu.VMEM((3, (KF + 1) * R, width), BF16),
            pltpu.VMEM((ROWS, width), BF16),
            pltpu.VMEM((R, 128), F32),
            pltpu.VMEM((2 * R, 1), F32),
            pltpu.VMEM((segs, 128), F32),
            pltpu.VMEM((count, segs, 128), F32),
            pltpu.VMEM((8, chans), F32),
            pltpu.VMEM((n_ctx, shard, chans), BF16),
            pltpu.VMEM((1, 8, chans), BF16),
            pltpu.VMEM((2, 8, chans), BF16),
            pltpu.VMEM((n_ctx, shard, half), BF16),
            pltpu.VMEM((n_ctx, shard, half), BF16),
            pltpu.VMEM((n_ctx, shard, half), BF16),
            pltpu.VMEM((shard, half), F32),
            pltpu.VMEM((1, 8, half), BF16),
            pltpu.VMEM((phases, 1, 8, half), BF16),
            pltpu.VMEM((1, 8, half), BF16),
            pltpu.VMEM((2, 8, half), BF16),
            pltpu.VMEM((phases, 2, 8, half), BF16),
            pltpu.VMEM((2, 8, half), BF16),
            pltpu.VMEM((3, KF, half), F32),
            dma((4 + len(TABLES),)),
            dma((2,)),
            dma((2, n_ctx)),
            dma((2, n_ctx)),
            dma((2, n_ctx)),
            dma((2,)),
            dma((2, blocks + 1)),
            dma((2, blocks)),
            dma((count,)),
            dma((count,)),
            dma((2, blocks)),
            dma((2, 3)),
            dma((2, n_ctx)),
            dma((2, 2, phases)),
            dma((2, 2)),
        ],
        compiler_params=pltpu.CompilerParams(
            collective_id=0, has_side_effects=True, vmem_limit_bytes=54 * 2**20
        ),
        name="hyena",
    )(
        seg_lengths, list_ids, score_dir[None, :], streams, feat_taps, long_filter, upstream,
        *[jnp.asarray(t, BF16) for t in TABLES],
    )
    return pl.pallas_call(
        store,
        in_specs=[hbm] * 3,
        out_specs=[hbm] * 3,
        out_shape=[
            jax.ShapeDtypeStruct((3, rows, chans), BF16),
            jax.ShapeDtypeStruct((3, KF, chans), F32),
            jax.ShapeDtypeStruct((shard, chans), F32),
        ],
        scratch_shapes=[dma((3,))],
        compiler_params=pltpu.CompilerParams(vmem_limit_bytes=2**20),
        name="store",
    )(d_streams, d_taps, d_filter)


def solution(mesh):
    placed = (
        P(None, ("groups", "ctx", "sub"), "fsdp"),
        P(None, None, "fsdp"),
        P("ctx", "fsdp"),
        P(("groups", "ctx", "sub"), "fsdp"),
        P("fsdp"),
        P("groups"),
        P("groups"),
    )
    sizes = (mesh.shape["ctx"], mesh.shape["fsdp"], mesh.shape["sub"])
    return jax.shard_map(
        functools.partial(local, sizes),
        mesh=mesh,
        in_specs=placed,
        out_specs=(
            P(None, ("groups", "ctx", "sub"), "fsdp"),
            P("groups", None, "fsdp"),
            P(("groups", "ctx"), "fsdp"),
        ),
        check_vma=False,
    )
```
